512 devices in a mesh: dp: 32 (over z, core), tensor: 16 (over y, x).
Axes of the slice: x: 4, y: 4, z: 16, core: 2. Of those that a mesh axis runs over, the one named last changes fastest.
Arguments:
- features: bfloat16 [40960, 2048], P(('dp', 'tensor')), may hold values from -6 to 6
- w_hidden: bfloat16 [2048, 2048], P(None, 'tensor'), may hold values from -0.125 to 0.125
- w_embed: bfloat16 [2048, 768], P('tensor'), may hold values from -0.125 to 0.125
- members: bfloat16 [32, 2048, 768], P('dp', 'tensor'), may hold values from -6 to 6
- doc_owner: int32 [40960, 1], P('dp'), may hold values from 0 to 31; in each aligned block of 80 rows (0 to 79, 80 to 159, ...) at most 5 rows name the same one
- doc_local: int32 [40960], P('dp'), may hold values from 0 to 15
- member_cluster: int32 [32, 2048], P('dp', 'tensor'), may hold values from 0 to 15, never falling along the last dimension, each value on 1 to 192 neighbouring positions
- member_valid: int32 [32, 2048], P('dp', 'tensor'), may hold values 0 or 1
Outputs:
- best: float32 [40960], P(('dp', 'tensor'))
The draws below stay inside these ranges and needn't reach their ends.
Inputs may be any that keep to these rules, and one draw needn't show every extreme that they name: Among the 80 documents of one device (aligned blocks of doc_owner's rows, in the order of dp then tensor) no owner is named more than 5 times; some owner is named exactly 5 times. `member_cluster`: along each owner's row the clusters never fall; every cluster has 1 to 192 slots.
All inputs are finite; a program needn't handle non-finite values. No bound on the sum of `member_valid` on one device may be relied on, other than what follows from the above.
Results may differ from the reference program's by a relative error of at most 0.013.
Values may be sent and summed in bfloat16 or wider, within the bound.
No kernel may reach another device: no remote copies, remote signals or barrier semaphores. Data moves between devices by JAX's collectives and lax.ppermute only.
A program may use at most 64 MiB of HBM per device.

```python
import math
import jax
import jax.numpy as jnp
import numpy as np
from jax import lax

HID = 2048
EMB = 768
DOC_TP = 80
CL_DEV = 16
CAP = 5
DOCS = 40960
MEM_OWN = 2048
N_DP = 32
N_TENSOR = 16


def place_ends(array, own_key, least, largest):
    longest = array.shape.index(max(array.shape))
    spots = []
    for shift in (0, 1):
        where = [jax.random.randint(jax.random.fold_in(own_key, axis), (), 0, length) for axis, length in enumerate(array.shape)]
        where[longest] = (where[longest] + shift) % array.shape[longest]
        spots.append(tuple(where))
    return array.at[spots[0]].set(least).at[spots[1]].set(largest)


def shard_levels(stream_key, extent, pieces, smallest, top_value):
    def one(dim, parts):
        draws = jax.random.uniform(jax.random.fold_in(jax.random.fold_in(stream_key, 6), dim), (parts,), jnp.float32, smallest / len(pieces), top_value / len(pieces))
        return jnp.repeat(jnp.exp(draws), extent[dim] // parts).reshape((-1,) + (1,) * (len(extent) - dim - 1))

    level = one(*pieces[0])
    for cut in pieces[1:]:
        level = level * one(*cut)
    return level


def length_profile(number_of, total, limit, lean):
    loads = [(1 << 20) // math.isqrt(grade ** lean) + 1 for grade in range(2, number_of + 1)]
    surplus, counts = total - limit - (number_of - 1), [1] * (number_of - 1)
    while surplus > 0:
        movable = [i for i in range(number_of - 1) if counts[i] < limit]
        pool, remaining = sum([loads[i] for i in movable]), surplus
        for i in movable:
            extra = min(limit - counts[i], max(1, remaining * loads[i] // pool), surplus)
            counts[i] = counts[i] + extra
            surplus = surplus - extra
    return np.array([limit] + counts)


def ragged_sizes(key, count, total, reach, skew):
    if count == 2:
        one = jax.random.randint(key, (), max(1, total - reach), min(reach, total - 1) + 1)
        return jnp.stack([one, total - one])
    sizes = jnp.asarray(length_profile(count, total, reach, skew), jnp.int32)
    pairs = (count - 1) // 2
    giver, sink = sizes[1:1 + 2 * pairs:2], sizes[2:2 + 2 * pairs:2]
    room = jnp.minimum(giver - 1, reach - sink)
    passed = jax.random.randint(jax.random.fold_in(key, 1), (pairs,), 0, 1 << 20) % (room + 1)
    sizes = sizes.at[1:1 + 2 * pairs:2].set(giver - passed).at[2:2 + 2 * pairs:2].set(sink + passed)
    return sizes[jax.random.permutation(jax.random.fold_in(key, 2), count)]


def routed_block(key, own, number, rows, amount, top, most, skew):
    sequence = jax.random.permutation(key, amount)
    crowded, usual = load_shares(amount, rows * top, most, skew, True), load_shares(amount, rows * top, most, skew, False)
    places = jnp.arange(amount)

    def named(lengths, rotation):
        used = int((lengths > 0).sum())
        fixed = max(1, used // 4)
        passed = fixed + (places - fixed + rotation * (used - fixed)) % max(1, amount - fixed)
        return jnp.zeros((amount,), jnp.int32).at[sequence[jnp.where(places < fixed, places, passed)]].set(jnp.asarray(lengths, jnp.int32))

    lengths = jnp.where(number % 4 == 0, named(crowded, number // 4), named(usual, number - number // 4 - 1))
    mixed = jax.random.permutation(jax.random.fold_in(own, 3), amount)
    source_of, receiver = mixed[0:amount // 2 * 2:2], mixed[1:amount // 2 * 2:2]
    room = jnp.minimum(lengths[source_of] - 1, most - lengths[receiver]) // 2
    room = jnp.where((source_of == sequence[0]) | (receiver == sequence[0]) | (lengths[receiver] == 0), 0, jnp.maximum(room, 0))
    passed = jax.random.randint(jax.random.fold_in(own, 4), (amount // 2,), 0, 1 << 20) % (room + 1)
    lengths = lengths.at[source_of].add(-passed).at[receiver].add(passed)
    labels = jnp.searchsorted(jnp.cumsum(lengths), jnp.arange(rows * top), side="right").astype(jnp.int32)
    table = labels.reshape(top, rows).T
    table = table[jax.random.permutation(jax.random.fold_in(own, 1), rows)]
    rotation = jax.random.randint(jax.random.fold_in(own, 2), (rows, 1), 0, top)
    return jnp.take_along_axis(table, (jnp.arange(top)[None, :] + rotation) % top, axis=1)


def load_shares(count, total, reach, lean, full):
    weights = [(1 << 20) // math.isqrt(standing ** lean) + 1 for standing in range(1, count + 1)]
    largest = reach if full else min(reach, max(-(-total // count), total * weights[0] // sum(weights)))
    least = 1 if total - largest >= count - 1 else 0
    counts, rest = [largest] + [least] * (count - 1), total - largest - least * (count - 1)
    while rest > 0:
        free = [i for i in range(1, count) if counts[i] < largest] or [i for i in range(1, count) if counts[i] < reach]
        mass, budget = sum([weights[i] for i in free]), rest
        for i in free:
            addition = min(reach - counts[i], max(1, budget * weights[i] // mass), rest)
            counts[i] = counts[i] + addition
            rest = rest - addition
    return np.array(counts)


def bell_draw(key, extent, scale, most, pieces=(), kind=jnp.bfloat16):
    array = scale * jax.random.normal(key, extent, jnp.float32)
    if pieces:
        array = array * shard_levels(key, extent, pieces, -0.22, 0.18)
    return jnp.clip(array, -most, most).astype(kind)


def setup_inputs(seed: int = 0) -> dict:
    seeds = jax.random.split(jax.random.key(seed), 9)
    features = bell_draw(seeds[0], (DOCS, HID), 1.0, 6.0, ((0, 512),))
    w_hidden = bell_draw(seeds[1], (HID, HID), HID ** -0.5, 0.125, ((1, 16),))
    w_embed = bell_draw(seeds[2], (HID, EMB), HID ** -0.5, 0.125, ((0, 16),))
    members = bell_draw(seeds[3], (N_DP, MEM_OWN, EMB), 1.0, 6.0, ((0, 32), (1, 16)))
    doc_owner_keys = jax.random.split(jax.random.fold_in(seeds[4], 1), DOCS // DOC_TP)
    doc_owner_turns = jax.random.permutation(jax.random.fold_in(seeds[4], 3), DOCS // DOC_TP)
    doc_owner = jax.vmap(lambda own, number: routed_block(jax.random.fold_in(seeds[4], 2), own, number, DOC_TP, N_DP, 1, CAP, 2))(doc_owner_keys, doc_owner_turns).reshape((DOCS, 1))
    doc_local = place_ends(jax.random.randint(seeds[5], (DOCS,), 0, CL_DEV), jax.random.fold_in(seeds[5], 1), 0, CL_DEV - 1).astype(jnp.int32)
    member_cluster = jax.vmap(lambda own: jnp.searchsorted(jnp.cumsum(ragged_sizes(own, CL_DEV, MEM_OWN, 3 * MEM_OWN // (2 * CL_DEV), 1)), jnp.arange(MEM_OWN), side="right"))(jax.random.split(seeds[6], N_DP)).reshape((N_DP, MEM_OWN)).astype(jnp.int32)
    member_valid = place_ends((jax.random.randint(seeds[7], (N_DP, MEM_OWN), 0, 4) < 3).astype(jnp.int32), jax.random.fold_in(seeds[7], 1), 0, 1)
    return dict(features=features, w_hidden=w_hidden, w_embed=w_embed, members=members, doc_owner=doc_owner, doc_local=doc_local, member_cluster=member_cluster, member_valid=member_valid)


epsilon = 1e-06

def unit_rows(vectors):
    values = vectors.astype(jnp.float32)
    return (values / jnp.sqrt(lax.optimization_barrier(jnp.sum(values * values, axis=-1, keepdims=True)) + epsilon)).astype(jnp.bfloat16)

def reference(features, w_hidden, w_embed, members, doc_owner, doc_local, member_cluster, member_valid):
    hidden = jax.nn.gelu(jnp.dot(features, w_hidden, preferred_element_type=jnp.float32)).astype(jnp.bfloat16)
    block_width = HID // N_TENSOR
    proj = jnp.zeros((DOCS, EMB), jnp.float32)
    for shard in range(N_TENSOR):
        part_rows = hidden[:, shard * block_width:(shard + 1) * block_width]
        part_weight = w_embed[shard * block_width:(shard + 1) * block_width, :]
        term = jnp.dot(part_rows, part_weight, preferred_element_type=jnp.float32).astype(jnp.bfloat16)
        proj = proj + term.astype(jnp.float32)
    query = unit_rows(proj)
    unit = unit_rows(members)
    owner = doc_owner[:, 0]
    onehot = (owner[:, None] == jnp.arange(N_DP, dtype=jnp.int32)[None, :]).astype(jnp.int32)
    ranking = lax.optimization_barrier(jnp.sum((jnp.cumsum(onehot, axis=0) - 1) * onehot, axis=1)).astype(jnp.int32)
    slot_width = N_DP * N_TENSOR * CAP
    table = jnp.full((N_DP, slot_width), DOCS, jnp.int32)
    table = table.at[owner, ranking].set(jnp.arange(DOCS, dtype=jnp.int32))

    def per_owner(owner_index):
        picks = table[owner_index]
        rows_here = jnp.take(query, picks, axis=0, mode='fill', fill_value=0)
        local_here = jnp.take(doc_local, picks, axis=0, mode='fill', fill_value=-1)
        scores = jnp.dot(rows_here.astype(jnp.float32), unit[owner_index].astype(jnp.float32).T)
        allowed = (member_valid[owner_index][None, :] == 1) & (member_cluster[owner_index][None, :] == local_here[:, None])
        return lax.optimization_barrier(jnp.max(jnp.where(allowed, scores, -1.0), axis=1))
    values = lax.map(per_owner, jnp.arange(N_DP, dtype=jnp.int32))
    best = jnp.full((DOCS,), -1.0, jnp.float32)
    return best.at[table.reshape(-1)].set(values.reshape(-1), mode='drop')
```

```python
import jax
import jax.numpy as jnp
import numpy as np
from jax import lax
from jax.experimental import pallas as pl
from jax.experimental.pallas import tpu as pltpu
from jax.sharding import Mesh, PartitionSpec as P

EPS = 1e-06
HID, EMB, ROWS, SLOTS, BLOCK, OWNERS, CAP = 2048, 768, 80, 128, 128, 32, 5
HALF = HID // 2
PACK = HALF + 3 * BLOCK
UNIT = SLOTS + 8
CHUNK = 256
LINES = 16
F32, BF16, I32 = jnp.float32, jnp.bfloat16, jnp.int32
PARAMS = pltpu.CompilerParams(vmem_limit_bytes=48 << 20)


def sds(shape, dtype):
    return jax.ShapeDtypeStruct(shape, dtype)


def iota(shape, dim):
    return lax.broadcasted_iota(I32, shape, dim)


def call(body, out, name, scalars=0):
    vm = pl.BlockSpec(memory_space=pltpu.VMEM)
    sm = pl.BlockSpec(memory_space=pltpu.SMEM)

    def run(*args):
        specs = [sm] * scalars + [vm] * (len(args) - scalars)
        outs = jax.tree.map(lambda _: vm, out)
        return pl.pallas_call(
            body, out_shape=out, in_specs=specs, out_specs=outs, name=name, compiler_params=PARAMS
        )(*args)

    return run


def unit_kernel(members, cluster, valid, out):
    values = members[0].astype(F32)
    norm = jnp.sum(values * values, axis=1, keepdims=True)
    out[0:SLOTS, :] = (values * (1.0 / jnp.sqrt(norm + EPS))).astype(BF16)
    tag = jnp.where(valid[...] == 1, cluster[...] + 1, 0).astype(F32)
    tag = jnp.concatenate([tag] * (EMB // SLOTS), axis=1)
    out[SLOTS:UNIT, :] = jnp.broadcast_to(tag, (8, EMB)).astype(BF16)


def weights_kernel(core, w_hidden, w_embed, out):
    c = core[0]
    upper = w_hidden[pl.ds(pl.multiple_of(c * HALF, HALF), HALF), :]
    for j in range(4):
        out[j, 0:HALF, :] = upper
    for i in range(3):
        piece = w_embed[:, pl.ds(pl.multiple_of(c * 3 * BLOCK + i * BLOCK, BLOCK), BLOCK)]
        for j in range(4):
            out[j, HALF + i * BLOCK : HALF + (i + 1) * BLOCK, :] = piece


def slots_kernel(owner_row, owner_col, local_col, place, tags, rank_row):
    row, col = owner_row[...], owner_col[...]
    same = row == col
    up, across = iota((ROWS, ROWS), 0), iota((ROWS, ROWS), 1)
    ranks = jnp.sum(jnp.where(same & (up < across), 1, 0), axis=0, keepdims=True)
    ranks_col = jnp.sum(jnp.where(same & (across < up), 1, 0), axis=1, keepdims=True)
    rank_row[...] = ranks
    line = iota((OWNERS * LINES, ROWS), 0)
    mine = row == line // LINES
    inner = line % LINES
    parts = [mine & (inner == k * CAP + ranks) for k in range(3)] + [mine & (inner == LINES - 1)]
    for k in range(4):
        place[k] = jnp.where(parts[k], 1.0, 0.0).astype(BF16)
    lane = iota((ROWS, CHUNK), 1)
    tags[...] = jnp.where(lane == ranks_col, local_col[...] + 1, 0).astype(F32).astype(BF16)


def head_kernel(features, weights, out):
    docs = features[...].reshape(4 * ROWS, HID)
    total = None
    for pair in range(2):
        a, b = 2 * pair, 2 * pair + 1
        pre = None
        for c in range(2):
            w = jnp.concatenate([weights[c, a, 0:HALF, :], weights[c, b, 0:HALF, :]], axis=1)
            part = jnp.dot(docs[:, c * HALF : (c + 1) * HALF], w, preferred_element_type=F32)
            pre = part if pre is None else pre + part
        hidden = jax.nn.gelu(pre).astype(BF16)
        rows = []
        for j in (a, b):
            rows.append(
                jnp.concatenate(
                    [
                        weights[c, j, HALF + i * BLOCK : HALF + (i + 1) * BLOCK, :]
                        for c in range(2)
                        for i in range(3)
                    ],
                    axis=1,
                )
            )
        part = jnp.dot(hidden, jnp.concatenate(rows, axis=0), preferred_element_type=F32)
        total = part if total is None else total + part
    out[...] = total.astype(BF16).reshape(4, ROWS, EMB)


def query_kernel(partial, place, tags, out):
    proj = partial[0].astype(F32)
    for j in range(1, 4):
        proj = proj + partial[j].astype(F32)
    norm = jnp.sum(proj * proj, axis=1, keepdims=True)
    query = (proj * (1.0 / jnp.sqrt(norm + EPS))).astype(BF16)
    total = jnp.dot(place[3], tags[...], preferred_element_type=F32)
    for k in range(3):
        total = total + jnp.dot(
            place[k], query[:, k * CHUNK : (k + 1) * CHUNK], preferred_element_type=F32
        )
    out[...] = total.astype(BF16).reshape(OWNERS, LINES, CHUNK)


def score_kernel(arrived, pick, unit, out):
    flat = arrived[...].reshape(OWNERS * LINES, CHUNK)
    moved = jnp.dot(pick[...], flat, preferred_element_type=F32)
    count = OWNERS * CAP
    query = jnp.concatenate(
        [moved[k * count : (k + 1) * count].astype(BF16) for k in range(3)], axis=1
    )
    slot = iota((count, CHUNK), 0) // OWNERS
    tag = jnp.sum(
        jnp.where(iota((count, CHUNK), 1) == slot, moved[3 * count :], 0.0), axis=1, keepdims=True
    )
    best = jnp.full((count, 2 * SLOTS), -1.0, F32)
    for j in range(0, 16, 2):
        blocks, marks = [], []
        for i in (j, j + 1):
            blocks.append(unit[i * UNIT : i * UNIT + SLOTS, :])
            marks.append(unit[i * UNIT + SLOTS : (i + 1) * UNIT, 0:SLOTS].astype(F32)[0:1])
        scores = lax.dot_general(
            query,
            jnp.concatenate(blocks, axis=0),
            (((1,), (1,)), ((), ())),
            preferred_element_type=F32,
        )
        allowed = jnp.concatenate(marks, axis=1) == tag
        best = jnp.maximum(best, jnp.where(allowed, scores, -1.0))
    best = jnp.max(best, axis=1, keepdims=True)
    lane = iota((OWNERS, SLOTS), 1)
    result = jnp.zeros((OWNERS, SLOTS), F32)
    for s in range(CAP):
        result = jnp.where(lane == s, best[s * OWNERS : (s + 1) * OWNERS], result)
    out[...] = result


def answer_kernel(answers, owner_row, rank_row, out):
    mine = owner_row[...] == iota((OWNERS, ROWS), 0)
    total = jnp.zeros((1, ROWS), F32)
    for s in range(CAP):
        value = jnp.sum(jnp.where(mine, answers[:, s : s + 1], 0.0), axis=0, keepdims=True)
        total = jnp.where(rank_row[...] == s, value, total)
    out[...] = total


def picking():
    count = OWNERS * CAP
    pick = np.zeros((4 * count, OWNERS * LINES), np.float32)
    for s in range(CAP):
        for o in range(OWNERS):
            for k in range(3):
                pick[k * count + s * OWNERS + o, o * LINES + k * CAP + s] = 1
            pick[3 * count + s * OWNERS + o, o * LINES + LINES - 1] = 1
    return jnp.asarray(pick, BF16)


def body(features, w_hidden, w_embed, members, doc_owner, doc_local, member_cluster, member_valid):
    dp = ("z", "core")
    unit = call(unit_kernel, sds((UNIT, EMB), BF16), "unit")(members, member_cluster, member_valid)
    units = lax.all_gather(unit, ("y", "x"), axis=0, tiled=True)

    core = lax.axis_index("core").astype(I32).reshape(1)
    half = call(weights_kernel, sds((4, PACK, BLOCK), BF16), "weights", 1)(core, w_hidden, w_embed)
    docs = lax.all_to_all(
        jnp.broadcast_to(features[None], (4, ROWS, HID)), "x", 0, 0, tiled=True
    )
    halves = lax.all_to_all(half, "y", 0, 0, tiled=True)
    weights = lax.all_to_all(
        jnp.broadcast_to(halves[None], (2, 4, PACK, BLOCK)), "core", 0, 0, tiled=True
    )

    first = lax.axis_index(("y", "x")) * ROWS
    owner = lax.dynamic_slice_in_dim(doc_owner[:, 0], first, ROWS, 0)
    local = lax.dynamic_slice_in_dim(doc_local, first, ROWS, 0)
    owner_row = owner.reshape(1, ROWS)
    place, tags, rank_row = call(
        slots_kernel,
        (
            sds((4, OWNERS * LINES, ROWS), BF16),
            sds((ROWS, CHUNK), BF16),
            sds((1, ROWS), I32),
        ),
        "slots",
    )(owner_row, owner.reshape(ROWS, 1), local.reshape(ROWS, 1))

    partial = call(head_kernel, sds((4, ROWS, EMB), BF16), "head")(docs, weights)
    partial = lax.all_to_all(partial, "x", 0, 0, tiled=True)
    outgoing = call(query_kernel, sds((OWNERS, LINES, CHUNK), BF16), "query")(partial, place, tags)
    arrived = lax.all_to_all(outgoing, dp, 0, 0, tiled=True)
    best = call(score_kernel, sds((OWNERS, SLOTS), F32), "score")(arrived, picking(), units)
    answers = lax.all_to_all(best, dp, 0, 0, tiled=True)
    result = call(answer_kernel, sds((1, ROWS), F32), "answer")(answers, owner_row, rank_row)
    return result.reshape(ROWS)


def solution(mesh):
    grid = Mesh(mesh.devices.reshape(16, 2, 4, 4), ("z", "core", "y", "x"))
    dp, tensor = ("z", "core"), ("y", "x")
    every = dp + tensor
    return jax.shard_map(
        body,
        mesh=grid,
        in_specs=(
            P(every, None),
            P(None, tensor),
            P(tensor, None),
            P(dp, tensor, None),
            P(dp, None),
            P(dp),
            P(dp, tensor),
            P(dp, tensor),
        ),
        out_specs=P(every),
        check_vma=False,
    )
```

```python
import jax
import jax.numpy as jnp
import numpy as np
from jax import lax
from jax.experimental import pallas as pl
from jax.experimental.pallas import tpu as pltpu
from jax.sharding import Mesh, PartitionSpec as P

EPS = 1e-06
HID, EMB, ROWS, SLOTS, BLOCK, OWNERS, CAP = 2048, 768, 80, 128, 128, 32, 5
HALF = HID // 2
PACK = HALF + 3 * BLOCK
CHUNK = 256
LINES = 16
UNIT = SLOTS + 8
PARTS = 4
F32, BF16, I32 = jnp.float32, jnp.bfloat16, jnp.int32
PARAMS = pltpu.CompilerParams(vmem_limit_bytes=16 << 20)


def sds(shape, dtype):
    return jax.ShapeDtypeStruct(shape, dtype)


def iota(shape, dim):
    return lax.broadcasted_iota(I32, shape, dim)


def call(body, out, name):
    vm = pl.BlockSpec(memory_space=pltpu.VMEM)

    def run(*args):
        specs = [vm] * len(args)
        outs = jax.tree.map(lambda _: vm, out)
        return pl.pallas_call(
            body, out_shape=out, in_specs=specs, out_specs=outs, name=name, compiler_params=PARAMS
        )(*args)

    return run


def prepare_kernel(
    w_hidden, w_embed, members, cluster, valid, half, unit, held, slots, live, sem, sems
):
    c = lax.axis_index("core")
    first = [
        pltpu.make_async_copy(members.at[0], held, sem.at[0]),
        pltpu.make_async_copy(cluster, slots, sem.at[1]),
        pltpu.make_async_copy(valid, live, sem.at[2]),
    ]
    rest = []
    for j in range(4):
        rest.append(
            pltpu.make_async_copy(
                w_hidden.at[pl.ds(pl.multiple_of(c * HALF, HALF), HALF), :],
                half.at[j, 0:HALF, :],
                sems.at[j, 3],
            )
        )
        for i in range(3):
            rest.append(
                pltpu.make_async_copy(
                    w_embed.at[:, pl.ds(pl.multiple_of((3 * c + i) * BLOCK, BLOCK), BLOCK)],
                    half.at[j, HALF + i * BLOCK : HALF + (i + 1) * BLOCK, :],
                    sems.at[j, i],
                )
            )
    for copy in first + rest:
        copy.start()
    for copy in first:
        copy.wait()
    values = held[...].astype(F32)
    norm = jnp.sum(values * values, axis=1, keepdims=True)
    unit[0:SLOTS, :] = (values * (1.0 / jnp.sqrt(norm + EPS))).astype(BF16)
    tag = jnp.where(live[...] == 1, slots[...] + 1, 0).astype(F32)
    tag = jnp.concatenate([tag] * (EMB // SLOTS), axis=1)
    unit[SLOTS:UNIT, :] = jnp.broadcast_to(tag, (8, EMB)).astype(BF16)
    for copy in rest:
        copy.wait()


def slots_kernel(owner_row, owner_col, local_col, mark, place, tags, rank_row):
    row, col = owner_row[...], owner_col[...]
    same = row == col
    up, across = iota((ROWS, ROWS), 0), iota((ROWS, ROWS), 1)
    ranks = jnp.sum(jnp.where(same & (up < across), 1, 0), axis=0, keepdims=True)
    ranks_col = jnp.sum(jnp.where(same & (across < up), 1, 0), axis=1, keepdims=True)
    rank_row[...] = ranks
    line = iota((OWNERS * LINES, ROWS), 0)
    mine = row == line // LINES
    inner = line % LINES
    parts = [mine & (inner == k * CAP + ranks) for k in range(3)] + [mine & (inner == LINES - 1)]
    for k in range(4):
        place[k] = jnp.where(parts[k], 1.0, 0.0).astype(BF16)
    lane = iota((ROWS, CHUNK), 1)
    tags[...] = jnp.where(lane == ranks_col, local_col[...] + 1, 0).astype(F32).astype(BF16)


def head_kernel(
    own, left, right, far, mine, other, own_out, left_out, right_out, far_out, docs, kept, sem
):
    c = lax.axis_index("core")
    copies = [
        pltpu.make_async_copy(part, docs.at[i * ROWS : (i + 1) * ROWS, :], sem.at[i + 1])
        for i, part in enumerate((own, left, right, far))
    ]
    for copy in copies:
        copy.start()
    for copy in copies:
        copy.wait()
    pre, embeds = None, []
    for half, weights in ((c, mine), (1 - c, other)):
        lines = docs[:, pl.ds(pl.multiple_of(half * HALF, HALF), HALF)]
        w = jnp.concatenate([weights[j, 0:HALF, :] for j in range(4)], axis=1)
        part = jnp.dot(lines, w, preferred_element_type=F32)
        pre = part if pre is None else pre + part
        rows = []
        for j in range(4):
            cut = [HALF + i * BLOCK for i in range(3)]
            rows.append(jnp.concatenate([weights[j, r : r + BLOCK, :] for r in cut], axis=1))
        embeds.append(jnp.concatenate(rows, axis=0))
    hidden = jax.nn.gelu(pre).astype(BF16)
    for k, embed in enumerate(embeds):
        total = jnp.dot(hidden, embed, preferred_element_type=F32)
        cut = slice(k * 3 * BLOCK, (k + 1) * 3 * BLOCK)
        kept[:, cut] = total[0:ROWS]
        for j, out in enumerate((left_out, right_out, far_out)):
            out[:, cut] = total[(j + 1) * ROWS : (j + 2) * ROWS].astype(BF16)
    copy = pltpu.make_async_copy(kept, own_out, sem.at[0])
    copy.start()
    copy.wait()


def query_kernel(own, left, right, far, place, tags, out, kept, sem):
    copy = pltpu.make_async_copy(own, kept, sem.at[0])
    copy.start()
    proj = left[...].astype(F32) + right[...].astype(F32) + far[...].astype(F32)
    copy.wait()
    proj = proj + kept[...]
    norm = jnp.sum(proj * proj, axis=1, keepdims=True)
    query = proj * (1.0 / jnp.sqrt(norm + EPS))
    low, high = query[:, 0 : EMB // 2], query[:, EMB // 2 :]
    straight = lax.axis_index("core") == 0
    query = jnp.concatenate(
        [jnp.where(straight, low, high), jnp.where(straight, high, low)], axis=1
    ).astype(BF16)
    total = jnp.dot(place[3], tags[...], preferred_element_type=F32)
    for k in range(3):
        total = total + jnp.dot(
            place[k], query[:, k * CHUNK : (k + 1) * CHUNK], preferred_element_type=F32
        )
    out[...] = total.astype(BF16).reshape(OWNERS, LINES, CHUNK)


def score_kernel(arrived, pick, units, out, held, sem):
    rows = 16 * UNIT // PARTS
    copies = [
        pltpu.make_async_copy(
            units.at[i * rows : (i + 1) * rows, :], held.at[i * rows : (i + 1) * rows, :], sem.at[i]
        )
        for i in range(PARTS)
    ]
    for copy in copies:
        copy.start()
    flat = arrived[...].reshape(OWNERS * LINES, CHUNK)
    moved = jnp.dot(pick[...], flat, preferred_element_type=F32)
    count = OWNERS * CAP
    query = jnp.concatenate(
        [moved[k * count : (k + 1) * count].astype(BF16) for k in range(3)], axis=1
    )
    slot = iota((count, CHUNK), 0) // OWNERS
    tag = jnp.sum(
        jnp.where(iota((count, CHUNK), 1) == slot, moved[3 * count :], 0.0), axis=1, keepdims=True
    )
    best = jnp.full((count, 2 * SLOTS), -1.0, F32)
    for j in range(0, 16, 2):
        if j % (16 // PARTS) == 0:
            copies[j // (16 // PARTS)].wait()
        blocks, marks = [], []
        for i in (j, j + 1):
            blocks.append(held[i * UNIT : i * UNIT + SLOTS, :])
            marks.append(held[i * UNIT + SLOTS : (i + 1) * UNIT, 0:SLOTS].astype(F32)[0:1])
        scores = lax.dot_general(
            query,
            jnp.concatenate(blocks, axis=0),
            (((1,), (1,)), ((), ())),
            preferred_element_type=F32,
        )
        allowed = jnp.concatenate(marks, axis=1) == tag
        best = jnp.maximum(best, jnp.where(allowed, scores, -1.0))
    best = jnp.max(best, axis=1, keepdims=True)
    lane = iota((OWNERS, SLOTS), 1)
    result = jnp.zeros((OWNERS, SLOTS), F32)
    for s in range(CAP):
        result = jnp.where(lane == s, best[s * OWNERS : (s + 1) * OWNERS], result)
    out[...] = result


def answer_kernel(answers, owner_row, rank_row, out):
    mine = owner_row[...] == iota((OWNERS, ROWS), 0)
    total = jnp.zeros((1, ROWS), F32)
    for s in range(CAP):
        value = jnp.sum(jnp.where(mine, answers[:, s : s + 1], 0.0), axis=0, keepdims=True)
        total = jnp.where(rank_row[...] == s, value, total)
    out[...] = total


def picking():
    count = OWNERS * CAP
    pick = np.zeros((4 * count, OWNERS * LINES), np.float32)
    for s in range(CAP):
        for o in range(OWNERS):
            for k in range(3):
                pick[k * count + s * OWNERS + o, o * LINES + k * CAP + s] = 1
            pick[3 * count + s * OWNERS + o, o * LINES + LINES - 1] = 1
    return jnp.asarray(pick, BF16)


def shift(value, axis, step):
    return lax.ppermute(value, axis, [(i, (i + step) % 4) for i in range(4)])


HBM = pl.BlockSpec(memory_space=pltpu.HBM)
VMEM = pl.BlockSpec(memory_space=pltpu.VMEM)


def prepared(*arrays):
    return pl.pallas_call(
        prepare_kernel,
        out_shape=(sds((4, PACK, BLOCK), BF16), sds((UNIT, EMB), BF16)),
        in_specs=[HBM] * 5,
        out_specs=(VMEM, VMEM),
        scratch_shapes=[
            pltpu.VMEM((SLOTS, EMB), BF16),
            pltpu.VMEM((1, SLOTS), I32),
            pltpu.VMEM((1, SLOTS), I32),
            pltpu.SemaphoreType.DMA((3,)),
            pltpu.SemaphoreType.DMA((4, 4)),
        ],
        name="prepare",
        compiler_params=PARAMS,
    )(*arrays)


KEPT = [pltpu.VMEM((ROWS, EMB), F32), pltpu.SemaphoreType.DMA((1,))]


def head(*arrays):
    piece = sds((ROWS, EMB), BF16)
    return pl.pallas_call(
        head_kernel,
        out_shape=(pltpu.HBM((ROWS, EMB), F32), piece, piece, piece),
        in_specs=[HBM] * 4 + [VMEM] * 2,
        out_specs=(HBM, VMEM, VMEM, VMEM),
        scratch_shapes=[
            pltpu.VMEM((4 * ROWS, HID), BF16),
            pltpu.VMEM((ROWS, EMB), F32),
            pltpu.SemaphoreType.DMA((5,)),
        ],
        name="head",
        compiler_params=PARAMS,
    )(*arrays)


def query(*arrays):
    return pl.pallas_call(
        query_kernel,
        out_shape=sds((OWNERS, LINES, CHUNK), BF16),
        in_specs=[HBM] + [VMEM] * 5,
        out_specs=VMEM,
        scratch_shapes=KEPT,
        name="query",
        compiler_params=PARAMS,
    )(*arrays)


def score(arrived, pick, units):
    return pl.pallas_call(
        score_kernel,
        out_shape=sds((OWNERS, SLOTS), F32),
        in_specs=[VMEM, VMEM, HBM],
        out_specs=VMEM,
        scratch_shapes=[pltpu.VMEM((16 * UNIT, EMB), BF16), pltpu.SemaphoreType.DMA((PARTS,))],
        name="score",
        compiler_params=PARAMS,
    )(arrived, pick, units)


def stay(value):
    return pltpu.with_memory_space_constraint(value, pltpu.HBM)


def swap(value):
    return lax.ppermute(value, "core", [(0, 1), (1, 0)])


def body(features, w_hidden, w_embed, members, doc_owner, doc_local, member_cluster, member_valid):
    dp = ("z", "core")
    steps = (1, -1, 2)
    half, unit = prepared(*map(stay, (w_hidden, w_embed, members, member_cluster, member_valid)))
    units = lax.all_gather(unit, ("y", "x"), axis=0, tiled=True)
    mine = lax.all_to_all(half, "y", 0, 0, tiled=True)
    docs = [shift(features, "x", k) for k in steps]
    mine, *docs = lax.optimization_barrier((mine, *docs))
    other = swap(mine)
    mark = swap(member_cluster)

    first = lax.axis_index(("y", "x")) * ROWS
    owner = lax.dynamic_slice_in_dim(doc_owner[:, 0], first, ROWS, 0)
    local = lax.dynamic_slice_in_dim(doc_local, first, ROWS, 0)
    owner_row = owner.reshape(1, ROWS)
    place, tags, rank_row = call(
        slots_kernel,
        (
            sds((4, OWNERS * LINES, ROWS), BF16),
            sds((ROWS, CHUNK), BF16),
            sds((1, ROWS), I32),
        ),
        "slots",
    )(owner_row, owner.reshape(ROWS, 1), local.reshape(ROWS, 1), mark)

    own, *parts = head(*map(stay, (features, *docs)), mine, other)
    parts = [shift(p, "x", -k) for p, k in zip(parts, steps)]
    outgoing = query(stay(own), *parts, place, tags)
    arrived = lax.all_to_all(outgoing, dp, 0, 0, tiled=True)
    best = score(arrived, picking(), stay(units))
    answers = lax.all_to_all(best, dp, 0, 0, tiled=True)
    result = call(answer_kernel, sds((1, ROWS), F32), "answer")(answers, owner_row, rank_row)
    return result.reshape(ROWS)


def solution(mesh):
    grid = Mesh(mesh.devices.reshape(16, 2, 4, 4), ("z", "core", "y", "x"))
    dp, tensor = ("z", "core"), ("y", "x")
    every = dp + tensor
    return jax.shard_map(
        body,
        mesh=grid,
        in_specs=(
            P(every, None),
            P(None, tensor),
            P(tensor, None),
            P(dp, tensor, None),
            P(dp, None),
            P(dp),
            P(dp, tensor),
            P(dp, tensor),
        ),
        out_specs=P(every),
        check_vma=False,
    )
```

```python
import jax
import jax.numpy as jnp
import numpy as np
from jax import lax
from jax.experimental import pallas as pl
from jax.experimental.pallas import tpu as pltpu
from jax.sharding import Mesh, PartitionSpec as P

EPS = 1e-06
HID, EMB, ROWS, SLOTS, BLOCK, OWNERS, CAP = 2048, 768, 80, 128, 128, 32, 5
HALF = HID // 2
PACK = HALF + 3 * BLOCK
CHUNK = 256
LINES = 16
UNIT = SLOTS + 8
PARTS = 4
F32, BF16, I32 = jnp.float32, jnp.bfloat16, jnp.int32
PARAMS = pltpu.CompilerParams(vmem_limit_bytes=16 << 20)


def sds(shape, dtype):
    return jax.ShapeDtypeStruct(shape, dtype)


def iota(shape, dim):
    return lax.broadcasted_iota(I32, shape, dim)


def call(body, out, name):
    vm = pl.BlockSpec(memory_space=pltpu.VMEM)

    def run(*args):
        specs = [vm] * len(args)
        outs = jax.tree.map(lambda _: vm, out)
        return pl.pallas_call(
            body, out_shape=out, in_specs=specs, out_specs=outs, name=name, compiler_params=PARAMS
        )(*args)

    return run


def prepare_kernel(
    w_hidden, w_embed, members, cluster, valid, half, unit, held, slots, live, sem, sems
):
    c = lax.axis_index("core")
    first = [
        pltpu.make_async_copy(members.at[0], held, sem.at[0]),
        pltpu.make_async_copy(cluster, slots, sem.at[1]),
        pltpu.make_async_copy(valid, live, sem.at[2]),
    ]
    rest = []
    for j in range(4):
        rest.append(
            pltpu.make_async_copy(
                w_hidden.at[pl.ds(pl.multiple_of(c * HALF, HALF), HALF), :],
                half.at[j, 0:HALF, :],
                sems.at[j, 3],
            )
        )
        for i in range(3):
            rest.append(
                pltpu.make_async_copy(
                    w_embed.at[:, pl.ds(pl.multiple_of((3 * c + i) * BLOCK, BLOCK), BLOCK)],
                    half.at[j, HALF + i * BLOCK : HALF + (i + 1) * BLOCK, :],
                    sems.at[j, i],
                )
            )
    for copy in first + rest:
        copy.start()
    for copy in first:
        copy.wait()
    values = held[...].astype(F32)
    norm = jnp.sum(values * values, axis=1, keepdims=True)
    unit[0:SLOTS, :] = (values * (1.0 / jnp.sqrt(norm + EPS))).astype(BF16)
    tag = jnp.where(live[...] == 1, slots[...] + 1, 0).astype(F32)
    tag = jnp.concatenate([tag] * (EMB // SLOTS), axis=1)
    unit[SLOTS:UNIT, :] = jnp.broadcast_to(tag, (8, EMB)).astype(BF16)
    for copy in rest:
        copy.wait()


def slots_kernel(owner_row, owner_col, local_col, place, tags, rank_row):
    row, col = owner_row[...], owner_col[...]
    same = row == col
    up, across = iota((ROWS, ROWS), 0), iota((ROWS, ROWS), 1)
    ranks = jnp.sum(jnp.where(same & (up < across), 1, 0), axis=0, keepdims=True)
    ranks_col = jnp.sum(jnp.where(same & (across < up), 1, 0), axis=1, keepdims=True)
    rank_row[...] = ranks
    line = iota((OWNERS * LINES, ROWS), 0)
    mine = row == line // LINES
    inner = line % LINES
    parts = [mine & (inner == k * CAP + ranks) for k in range(3)] + [mine & (inner == LINES - 1)]
    for k in range(4):
        place[k] = jnp.where(parts[k], 1.0, 0.0).astype(BF16)
    lane = iota((ROWS, CHUNK), 1)
    tags[...] = jnp.where(lane == ranks_col, local_col[...] + 1, 0).astype(F32).astype(BF16)


def first_kernel(own, left, right, far_a, far_b, mine, pre, rest, docs, sem):
    c = lax.axis_index("core")
    copies, row = [], 0
    for i, part in enumerate((own, left, right, far_a, far_b)):
        rows = part.shape[0]
        copies.append(pltpu.make_async_copy(part, docs.at[row : row + rows, :], sem.at[i]))
        row += rows
    for copy in copies:
        copy.start()
    w = jnp.concatenate([mine[j, 0:HALF, :] for j in range(4)], axis=1)
    for copy in copies:
        copy.wait()
    lines = docs[:, pl.ds(pl.multiple_of(c * HALF, HALF), HALF)]
    pre[...] = jnp.dot(lines, w, preferred_element_type=F32)
    rest[...] = docs[:, pl.ds(pl.multiple_of((1 - c) * HALF, HALF), HALF)]


def head_kernel(pre, rest, mine, other, out):
    x = lax.axis_index("x")
    w = jnp.concatenate([other[j, 0:HALF, :] for j in range(4)], axis=1)
    total = pre[...] + jnp.dot(rest[...], w, preferred_element_type=F32)
    hidden = jax.nn.gelu(total).astype(BF16)
    for k, weights in enumerate((mine, other)):
        rows = []
        for j in range(4):
            cut = [HALF + i * BLOCK for i in range(3)]
            rows.append(jnp.concatenate([weights[j, r : r + BLOCK, :] for r in cut], axis=1))
        total = jnp.dot(hidden, jnp.concatenate(rows, axis=0), preferred_element_type=F32)
        cut = slice(k * 3 * BLOCK, (k + 1) * 3 * BLOCK)
        for j, step in enumerate((0, 3, 1, 2)):
            out[lax.rem(x + step, 4), :, cut] = total[j * ROWS : (j + 1) * ROWS].astype(BF16)


def query_kernel(partial, place, tags, out):
    proj = partial[0].astype(F32)
    for j in range(1, 4):
        proj = proj + partial[j].astype(F32)
    norm = jnp.sum(proj * proj, axis=1, keepdims=True)
    query = proj * (1.0 / jnp.sqrt(norm + EPS))
    low, high = query[:, 0 : EMB // 2], query[:, EMB // 2 :]
    straight = lax.axis_index("core") == 0
    query = jnp.concatenate(
        [jnp.where(straight, low, high), jnp.where(straight, high, low)], axis=1
    ).astype(BF16)
    total = jnp.dot(place[3], tags[...], preferred_element_type=F32)
    for k in range(3):
        total = total + jnp.dot(
            place[k], query[:, k * CHUNK : (k + 1) * CHUNK], preferred_element_type=F32
        )
    out[...] = total.astype(BF16).reshape(OWNERS, LINES, CHUNK)


def score_kernel(arrived, pick, units, out, held, sem):
    rows = 16 * UNIT // PARTS
    copies = [
        pltpu.make_async_copy(
            units.at[i * rows : (i + 1) * rows, :], held.at[i * rows : (i + 1) * rows, :], sem.at[i]
        )
        for i in range(PARTS)
    ]
    for copy in copies:
        copy.start()
    flat = arrived[...].reshape(OWNERS * LINES, CHUNK)
    moved = jnp.dot(pick[...], flat, preferred_element_type=F32)
    count = OWNERS * CAP
    query = jnp.concatenate(
        [moved[k * count : (k + 1) * count].astype(BF16) for k in range(3)], axis=1
    )
    slot = iota((count, CHUNK), 0) // OWNERS
    tag = jnp.sum(
        jnp.where(iota((count, CHUNK), 1) == slot, moved[3 * count :], 0.0), axis=1, keepdims=True
    )
    best = jnp.full((count, 2 * SLOTS), -1.0, F32)
    for j in range(0, 16, 2):
        if j % (16 // PARTS) == 0:
            copies[j // (16 // PARTS)].wait()
        blocks, marks = [], []
        for i in (j, j + 1):
            blocks.append(held[i * UNIT : i * UNIT + SLOTS, :])
            marks.append(held[i * UNIT + SLOTS : (i + 1) * UNIT, 0:SLOTS].astype(F32)[0:1])
        scores = lax.dot_general(
            query,
            jnp.concatenate(blocks, axis=0),
            (((1,), (1,)), ((), ())),
            preferred_element_type=F32,
        )
        allowed = jnp.concatenate(marks, axis=1) == tag
        best = jnp.maximum(best, jnp.where(allowed, scores, -1.0))
    best = jnp.max(best, axis=1, keepdims=True)
    lane = iota((OWNERS, SLOTS), 1)
    result = jnp.zeros((OWNERS, SLOTS), F32)
    for s in range(CAP):
        result = jnp.where(lane == s, best[s * OWNERS : (s + 1) * OWNERS], result)
    out[...] = result


def picking():
    count = OWNERS * CAP
    pick = np.zeros((4 * count, OWNERS * LINES), np.float32)
    for s in range(CAP):
        for o in range(OWNERS):
            for k in range(3):
                pick[k * count + s * OWNERS + o, o * LINES + k * CAP + s] = 1
            pick[3 * count + s * OWNERS + o, o * LINES + LINES - 1] = 1
    return jnp.asarray(pick, BF16)


def answer_kernel(answers, owner_row, rank_row, out):
    mine = owner_row[...] == iota((OWNERS, ROWS), 0)
    total = jnp.zeros((1, ROWS), F32)
    for s in range(CAP):
        value = jnp.sum(jnp.where(mine, answers[:, s : s + 1], 0.0), axis=0, keepdims=True)
        total = jnp.where(rank_row[...] == s, value, total)
    out[...] = total


def shift(value, axis, step):
    return lax.ppermute(value, axis, [(i, (i + step) % 4) for i in range(4)])


HBM = pl.BlockSpec(memory_space=pltpu.HBM)
VMEM = pl.BlockSpec(memory_space=pltpu.VMEM)


def prepared(*arrays):
    return pl.pallas_call(
        prepare_kernel,
        out_shape=(pltpu.VMEM((4, PACK, BLOCK), BF16), sds((UNIT, EMB), BF16)),
        in_specs=[HBM] * 5,
        out_specs=(VMEM, VMEM),
        scratch_shapes=[
            pltpu.VMEM((SLOTS, EMB), BF16),
            pltpu.VMEM((1, SLOTS), I32),
            pltpu.VMEM((1, SLOTS), I32),
            pltpu.SemaphoreType.DMA((3,)),
            pltpu.SemaphoreType.DMA((4, 4)),
        ],
        name="prepare",
        compiler_params=PARAMS,
    )(*arrays)


def score(arrived, pick, units):
    return pl.pallas_call(
        score_kernel,
        out_shape=sds((OWNERS, SLOTS), F32),
        in_specs=[VMEM, VMEM, HBM],
        out_specs=VMEM,
        scratch_shapes=[pltpu.VMEM((16 * UNIT, EMB), BF16), pltpu.SemaphoreType.DMA((PARTS,))],
        name="score",
        compiler_params=PARAMS,
    )(arrived, pick, units)


def first(*arrays):
    return pl.pallas_call(
        first_kernel,
        out_shape=(pltpu.VMEM((4 * ROWS, 4 * BLOCK), F32), pltpu.VMEM((4 * ROWS, HALF), BF16)),
        in_specs=[HBM] * 5 + [VMEM],
        out_specs=(VMEM, VMEM),
        scratch_shapes=[pltpu.VMEM((4 * ROWS, HID), BF16), pltpu.SemaphoreType.DMA((5,))],
        name="first",
        compiler_params=PARAMS,
    )(*arrays)


def near(value):
    return pltpu.with_memory_space_constraint(value, pltpu.VMEM)


def stay(value):
    return pltpu.with_memory_space_constraint(value, pltpu.HBM)


def swap(value):
    return lax.ppermute(value, "core", [(0, 1), (1, 0)])


def body(features, w_hidden, w_embed, members, doc_owner, doc_local, member_cluster, member_valid):
    dp = ("z", "core")
    half, unit = prepared(*map(stay, (w_hidden, w_embed, members, member_cluster, member_valid)))
    units = lax.all_gather(unit, ("y", "x"), axis=0, tiled=True)
    mine = lax.all_to_all(near(half), "y", 0, 0, tiled=True)
    left, right = shift(features, "x", 1), shift(features, "x", -1)
    cut = 48
    docs = [left, right, shift(left[:cut], "x", 1), shift(right[cut:], "x", -1)]

    start = lax.axis_index(("y", "x")) * ROWS
    owner = lax.dynamic_slice_in_dim(doc_owner[:, 0], start, ROWS, 0)
    local = lax.dynamic_slice_in_dim(doc_local, start, ROWS, 0)
    owner_row = owner.reshape(1, ROWS)
    place, tags, rank_row = call(
        slots_kernel,
        (
            pltpu.VMEM((4, OWNERS * LINES, ROWS), BF16),
            pltpu.VMEM((ROWS, CHUNK), BF16),
            sds((1, ROWS), I32),
        ),
        "slots",
    )(owner_row, owner.reshape(ROWS, 1), local.reshape(ROWS, 1))

    mine, place, *docs = lax.optimization_barrier((mine, place, *docs))
    other = swap(mine)
    pre, rest = first(*map(stay, (features, *docs)), mine)
    partial = call(head_kernel, sds((4, ROWS, EMB), BF16), "head")(near(pre), near(rest), mine, other)
    partial = lax.all_to_all(partial, "x", 0, 0, tiled=True)
    outgoing = call(query_kernel, sds((OWNERS, LINES, CHUNK), BF16), "query")(
        partial, near(place), near(tags)
    )
    arrived = lax.all_to_all(outgoing, dp, 0, 0, tiled=True)
    best = score(arrived, picking(), stay(units))
    answers = lax.all_to_all(best, dp, 0, 0, tiled=True)
    result = call(answer_kernel, sds((1, ROWS), F32), "answer")(answers, owner_row, rank_row)
    return result.reshape(ROWS)


def solution(mesh):
    grid = Mesh(mesh.devices.reshape(16, 2, 4, 4), ("z", "core", "y", "x"))
    dp, tensor = ("z", "core"), ("y", "x")
    every = dp + tensor
    return jax.shard_map(
        body,
        mesh=grid,
        in_specs=(
            P(every, None),
            P(None, tensor),
            P(tensor, None),
            P(dp, tensor, None),
            P(dp, None),
            P(dp),
            P(dp, tensor),
            P(dp, tensor),
        ),
        out_specs=P(every),
        check_vma=False,
    )
```

```python
import jax
import jax.numpy as jnp
import numpy as np
from jax import lax
from jax.experimental import pallas as pl
from jax.experimental.pallas import tpu as pltpu
from jax.sharding import Mesh, PartitionSpec as P

EPS = 1e-06
HID, EMB, ROWS, SLOTS, BLOCK, OWNERS, CAP = 2048, 768, 80, 128, 128, 32, 5
HALF = HID // 2
PACK = HALF + 3 * BLOCK
CHUNK = 256
LINES = 16
UNIT = SLOTS + 16
F32, BF16, I32 = jnp.float32, jnp.bfloat16, jnp.int32
PARAMS = pltpu.CompilerParams(vmem_limit_bytes=16 << 20)


def sds(shape, dtype):
    return jax.ShapeDtypeStruct(shape, dtype)


def iota(shape, dim):
    return lax.broadcasted_iota(I32, shape, dim)


def call(body, out, name):
    vm = pl.BlockSpec(memory_space=pltpu.VMEM)

    def run(*args):
        specs = [vm] * len(args)
        outs = jax.tree.map(lambda _: vm, out)
        return pl.pallas_call(
            body, out_shape=out, in_specs=specs, out_specs=outs, name=name, compiler_params=PARAMS
        )(*args)

    return run


def prepare_kernel(
    w_hidden, w_embed, members, cluster, valid, half, unit, held, slots, live, upper, lower, sem, sems
):
    c = lax.axis_index("core")
    first = [
        pltpu.make_async_copy(members.at[0], held, sem.at[0]),
        pltpu.make_async_copy(cluster, slots, sem.at[1]),
        pltpu.make_async_copy(valid, live, sem.at[2]),
    ]
    rest = [
        pltpu.make_async_copy(
            w_hidden.at[pl.ds(pl.multiple_of(c * HALF, HALF), HALF), :], upper, sems.at[0]
        ),
        pltpu.make_async_copy(
            w_embed.at[:, pl.ds(pl.multiple_of(c * 3 * BLOCK, BLOCK), 3 * BLOCK)], lower, sems.at[1]
        ),
    ]
    for copy in first + rest:
        copy.start()
    for copy in first:
        copy.wait()
    values = held[...].astype(F32)
    norm = jnp.sum(values * values, axis=1, keepdims=True)
    unit[0:SLOTS, :] = (values * (1.0 / jnp.sqrt(norm + EPS))).astype(BF16)
    tag = jnp.where(live[...] == 1, slots[...] + 1, 0).astype(F32)
    tag = jnp.concatenate([tag] * (EMB // SLOTS), axis=1)
    unit[SLOTS:UNIT, :] = jnp.broadcast_to(tag, (UNIT - SLOTS, EMB)).astype(BF16)
    for copy in rest:
        copy.wait()
    for j in range(4):
        half[j, 0:HALF, :] = upper[...]
        for i in range(3):
            half[j, HALF + i * BLOCK : HALF + (i + 1) * BLOCK, :] = lower[
                :, i * BLOCK : (i + 1) * BLOCK
            ]


def slots_kernel(owner_row, owner_col, local_col, tags, rank_row):
    row, col = owner_row[...], owner_col[...]
    same = row == col
    up, across = iota((ROWS, ROWS), 0), iota((ROWS, ROWS), 1)
    ranks = jnp.sum(jnp.where(same & (up < across), 1, 0), axis=0, keepdims=True)
    ranks_col = jnp.sum(jnp.where(same & (across < up), 1, 0), axis=1, keepdims=True)
    rank_row[...] = ranks
    lane = iota((ROWS, CHUNK), 1)
    tags[...] = jnp.where(lane == ranks_col, local_col[...] + 1, 0).astype(F32).astype(BF16)


def first_kernel(own, left, right, far_a, far_b, mine, pre, rest, docs, sem):
    c = lax.axis_index("core")
    copies, row = [], 0
    for i, part in enumerate((own, left, right, far_a, far_b)):
        rows = part.shape[0]
        copies.append(pltpu.make_async_copy(part, docs.at[row : row + rows, :], sem.at[i]))
        row += rows
    for copy in copies:
        copy.start()
    w = jnp.concatenate([mine[j, 0:HALF, :] for j in range(4)], axis=1)
    for copy in copies:
        copy.wait()
    lines = docs[:, pl.ds(pl.multiple_of(c * HALF, HALF), HALF)]
    pre[...] = jnp.dot(lines, w, preferred_element_type=F32)
    rest[...] = docs[:, pl.ds(pl.multiple_of((1 - c) * HALF, HALF), HALF)]


def head_kernel(pre, rest, mine, other, out):
    x = lax.axis_index("x")
    w = jnp.concatenate([other[j, 0:HALF, :] for j in range(4)], axis=1)
    total = pre[...] + jnp.dot(rest[...], w, preferred_element_type=F32)
    hidden = jax.nn.gelu(total).astype(BF16)
    for k, weights in enumerate((mine, other)):
        rows = []
        for j in range(4):
            cut = [HALF + i * BLOCK for i in range(3)]
            rows.append(jnp.concatenate([weights[j, r : r + BLOCK, :] for r in cut], axis=1))
        total = jnp.dot(hidden, jnp.concatenate(rows, axis=0), preferred_element_type=F32)
        cut = slice(k * 3 * BLOCK, (k + 1) * 3 * BLOCK)
        for j, step in enumerate((0, 3, 1, 2)):
            out[lax.rem(x + step, 4), :, cut] = total[j * ROWS : (j + 1) * ROWS].astype(BF16)


def query_kernel(partial, owner_row, rank_row, tags, out):
    line = iota((OWNERS * LINES, ROWS), 0)
    inner = jnp.where(owner_row[...] == line // LINES, line % LINES, -1)
    place = [
        jnp.where(inner == (k * CAP + rank_row[...] if k < 3 else LINES - 1), 1.0, 0.0).astype(BF16)
        for k in range(4)
    ]
    proj = partial[0].astype(F32)
    for j in range(1, 4):
        proj = proj + partial[j].astype(F32)
    norm = jnp.sum(proj * proj, axis=1, keepdims=True)
    query = proj * (1.0 / jnp.sqrt(norm + EPS))
    low, high = query[:, 0 : EMB // 2], query[:, EMB // 2 :]
    straight = lax.axis_index("core") == 0
    query = jnp.concatenate(
        [jnp.where(straight, low, high), jnp.where(straight, high, low)], axis=1
    ).astype(BF16)
    total = jnp.dot(place[3], tags[...], preferred_element_type=F32)
    for k in range(3):
        total = total + jnp.dot(
            place[k], query[:, k * CHUNK : (k + 1) * CHUNK], preferred_element_type=F32
        )
    out[...] = total.astype(BF16).reshape(OWNERS, LINES, CHUNK)


def column_kernel(own, left, right, far, out):
    for i, part in enumerate((own, left, right, far)):
        out[i * UNIT : (i + 1) * UNIT, :] = part[...]


def score_kernel(arrived, own, left, right, top, bottom, out, held, sem):
    copies = [
        pltpu.make_async_copy(top, held.at[0 : 2 * UNIT, :], sem.at[0]),
        pltpu.make_async_copy(bottom, held.at[2 * UNIT :, :], sem.at[1]),
    ]
    for copy in copies:
        copy.start()
    parts = (own, left, right, held)
    row = iota((4 * OWNERS * CAP, 1), 0)
    kind, slot = row // (OWNERS * CAP), row % (OWNERS * CAP)
    line = jnp.where(kind < 3, kind * CAP + slot // OWNERS, LINES - 1)
    target = slot % OWNERS * LINES + line
    pick = jnp.where(iota((4 * OWNERS * CAP, OWNERS * LINES), 1) == target, 1.0, 0.0).astype(BF16)
    flat = arrived[...].reshape(OWNERS * LINES, CHUNK)
    moved = jnp.dot(pick, flat, preferred_element_type=F32)
    count = OWNERS * CAP
    query = jnp.concatenate(
        [moved[k * count : (k + 1) * count].astype(BF16) for k in range(3)], axis=1
    )
    slot = iota((count, CHUNK), 0) // OWNERS
    tag = jnp.sum(
        jnp.where(iota((count, CHUNK), 1) == slot, moved[3 * count :], 0.0), axis=1, keepdims=True
    )
    best = jnp.full((count, 2 * SLOTS), -1.0, F32)
    where = [(part, i * UNIT) for part in parts for i in range(part.shape[0] // UNIT)]
    for j in range(0, 16, 2):
        if j == 12:
            for copy in copies:
                copy.wait()
        blocks, marks = [], []
        for part, row in where[j : j + 2]:
            blocks.append(part[row : row + SLOTS, :])
            marks.append(part[row + SLOTS : row + UNIT, 0:SLOTS].astype(F32)[0:1])
        scores = lax.dot_general(
            query,
            jnp.concatenate(blocks, axis=0),
            (((1,), (1,)), ((), ())),
            preferred_element_type=F32,
        )
        allowed = jnp.concatenate(marks, axis=1) == tag
        best = jnp.maximum(best, jnp.where(allowed, scores, -1.0))
    best = jnp.max(best, axis=1, keepdims=True)
    lane = iota((OWNERS, SLOTS), 1)
    result = jnp.zeros((OWNERS, SLOTS), F32)
    for s in range(CAP):
        result = jnp.where(lane == s, best[s * OWNERS : (s + 1) * OWNERS], result)
    out[...] = result


def answer_kernel(answers, owner_row, rank_row, out):
    mine = owner_row[...] == iota((OWNERS, ROWS), 0)
    total = jnp.zeros((1, ROWS), F32)
    for s in range(CAP):
        value = jnp.sum(jnp.where(mine, answers[:, s : s + 1], 0.0), axis=0, keepdims=True)
        total = jnp.where(rank_row[...] == s, value, total)
    out[...] = total


def shift(value, axis, step):
    return lax.ppermute(value, axis, [(i, (i + step) % 4) for i in range(4)])


def turn(value, step, turned):
    pairs = []
    for c in range(2):
        for y in range(4):
            for x in range(4):
                to = (y, (x + step) % 4) if (c == 1) == turned else ((y + step) % 4, x)
                pairs.append((c * 16 + y * 4 + x, c * 16 + to[0] * 4 + to[1]))
    return lax.ppermute(value, ("core", "y", "x"), pairs)


def gather(value, turned):
    return [value] + [turn(value, step, turned) for step in (1, -1, 2)]


HBM = pl.BlockSpec(memory_space=pltpu.HBM)
VMEM = pl.BlockSpec(memory_space=pltpu.VMEM)


def prepared(*arrays):
    return pl.pallas_call(
        prepare_kernel,
        out_shape=(pltpu.VMEM((4, PACK, BLOCK), BF16), sds((UNIT, EMB), BF16)),
        in_specs=[HBM] * 5,
        out_specs=(VMEM, VMEM),
        scratch_shapes=[
            pltpu.VMEM((SLOTS, EMB), BF16),
            pltpu.VMEM((1, SLOTS), I32),
            pltpu.VMEM((1, SLOTS), I32),
            pltpu.VMEM((HALF, BLOCK), BF16),
            pltpu.VMEM((BLOCK, 3 * BLOCK), BF16),
            pltpu.SemaphoreType.DMA((3,)),
            pltpu.SemaphoreType.DMA((2,)),
        ],
        name="prepare",
        compiler_params=PARAMS,
    )(*arrays)


def first(*arrays):
    return pl.pallas_call(
        first_kernel,
        out_shape=(pltpu.VMEM((4 * ROWS, 4 * BLOCK), F32), pltpu.VMEM((4 * ROWS, HALF), BF16)),
        in_specs=[HBM] * 5 + [VMEM],
        out_specs=(VMEM, VMEM),
        scratch_shapes=[pltpu.VMEM((4 * ROWS, HID), BF16), pltpu.SemaphoreType.DMA((5,))],
        name="first",
        compiler_params=PARAMS,
    )(*arrays)


def near(value):
    return pltpu.with_memory_space_constraint(value, pltpu.VMEM)


def score(*arrays):
    return pl.pallas_call(
        score_kernel,
        out_shape=sds((OWNERS, SLOTS), F32),
        in_specs=[VMEM] * 4 + [HBM] * 2,
        out_specs=VMEM,
        scratch_shapes=[pltpu.VMEM((4 * UNIT, EMB), BF16), pltpu.SemaphoreType.DMA((2,))],
        name="score",
        compiler_params=PARAMS,
    )(*arrays)


def stay(value):
    return pltpu.with_memory_space_constraint(value, pltpu.HBM)


def swap(value):
    return lax.ppermute(value, "core", [(0, 1), (1, 0)])


def body(features, w_hidden, w_embed, members, doc_owner, doc_local, member_cluster, member_valid):
    dp = ("z", "core")
    half, unit = prepared(*map(stay, (w_hidden, w_embed, members, member_cluster, member_valid)))
    units = gather(unit, False)
    mine = lax.all_to_all(near(half), "y", 0, 0, tiled=True)
    docs = [shift(features, "x", 1), shift(features, "x", -1)]
    cut = 48
    docs += [shift(docs[0][:cut], "x", 1), shift(docs[1][cut:], "x", -1)]

    start = lax.axis_index(("y", "x")) * ROWS
    owner = lax.dynamic_slice_in_dim(doc_owner[:, 0], start, ROWS, 0)
    local = lax.dynamic_slice_in_dim(doc_local, start, ROWS, 0)
    owner_row = owner.reshape(1, ROWS)
    tags, rank_row = call(
        slots_kernel,
        (
            sds((ROWS, CHUNK), BF16),
            sds((1, ROWS), I32),
        ),
        "slots",
    )(owner_row, owner.reshape(ROWS, 1), local.reshape(ROWS, 1))

    mine, tags, docs, units[1:] = lax.optimization_barrier((mine, tags, docs, units[1:]))
    other = swap(mine)
    column = call(column_kernel, sds((4 * UNIT, EMB), BF16), "column")(*map(near, units))
    left, right = turn(column, 1, True), turn(column, -1, True)
    top, bottom = turn(left[: 2 * UNIT], 1, True), turn(right[2 * UNIT :], -1, True)
    columns = [column, left, right, top, bottom]
    pre, rest = first(*map(stay, (features, *docs)), mine)
    partial = call(head_kernel, sds((4, ROWS, EMB), BF16), "head")(near(pre), near(rest), mine, other)
    partial = lax.all_to_all(partial, "x", 0, 0, tiled=True)
    outgoing = call(query_kernel, sds((OWNERS, LINES, CHUNK), BF16), "query")(
        partial, owner_row, rank_row, tags
    )
    arrived = lax.all_to_all(outgoing, dp, 0, 0, tiled=True)
    best = score(arrived, *map(near, columns[:3]), *map(stay, columns[3:]))
    answers = lax.all_to_all(best, dp, 0, 0, tiled=True)
    result = call(answer_kernel, sds((1, ROWS), F32), "answer")(answers, owner_row, rank_row)
    return result.reshape(ROWS)


def solution(mesh):
    grid = Mesh(mesh.devices.reshape(16, 2, 4, 4), ("z", "core", "y", "x"))
    dp, tensor = ("z", "core"), ("y", "x")
    every = dp + tensor
    return jax.shard_map(
        body,
        mesh=grid,
        in_specs=(
            P(every, None),
            P(None, tensor),
            P(tensor, None),
            P(dp, tensor, None),
            P(dp, None),
            P(dp),
            P(dp, tensor),
            P(dp, tensor),
        ),
        out_specs=P(every),
        check_vma=False,
    )
```

```python
import jax
import jax.numpy as jnp
import numpy as np
from jax import lax
from jax.experimental import pallas as pl
from jax.experimental.pallas import tpu as pltpu
from jax.sharding import Mesh, PartitionSpec as P

EPS = 1e-06
HID, EMB, ROWS, SLOTS, BLOCK, OWNERS, CAP = 2048, 768, 80, 128, 128, 32, 5
HALF = HID // 2
PACK = HALF + 3 * BLOCK
CHUNK = 256
LINES = 16
UNIT = SLOTS + 16
F32, BF16, I32 = jnp.float32, jnp.bfloat16, jnp.int32
PARAMS = pltpu.CompilerParams(vmem_limit_bytes=16 << 20)


def sds(shape, dtype):
    return jax.ShapeDtypeStruct(shape, dtype)


def iota(shape, dim):
    return lax.broadcasted_iota(I32, shape, dim)


def call(body, out, name):
    vm = pl.BlockSpec(memory_space=pltpu.VMEM)

    def run(*args):
        specs = [vm] * len(args)
        outs = jax.tree.map(lambda _: vm, out)
        return pl.pallas_call(
            body, out_shape=out, in_specs=specs, out_specs=outs, name=name, compiler_params=PARAMS
        )(*args)

    return run


def weights_kernel(w_hidden, w_embed, half, upper, lower, sem):
    c = lax.axis_index("core")
    copies = [
        pltpu.make_async_copy(
            w_hidden.at[pl.ds(pl.multiple_of(c * HALF, HALF), HALF), :], upper, sem.at[0]
        ),
        pltpu.make_async_copy(
            w_embed.at[:, pl.ds(pl.multiple_of(c * 3 * BLOCK, BLOCK), 3 * BLOCK)], lower, sem.at[1]
        ),
    ]
    for copy in copies:
        copy.start()
    for copy in copies:
        copy.wait()
    for j in range(4):
        half[j, 0:HALF, :] = upper[...]
        for i in range(3):
            half[j, HALF + i * BLOCK : HALF + (i + 1) * BLOCK, :] = lower[
                :, i * BLOCK : (i + 1) * BLOCK
            ]


def unit_kernel(members, cluster, valid, unit, held, slots, live, sem):
    copies = [
        pltpu.make_async_copy(members.at[0], held, sem.at[0]),
        pltpu.make_async_copy(cluster, slots, sem.at[1]),
        pltpu.make_async_copy(valid, live, sem.at[2]),
    ]
    for copy in copies:
        copy.start()
    for copy in copies:
        copy.wait()
    values = held[...].astype(F32)
    norm = jnp.sum(values * values, axis=1, keepdims=True)
    unit[0:SLOTS, :] = (values * (1.0 / jnp.sqrt(norm + EPS))).astype(BF16)
    tag = jnp.where(live[...] == 1, slots[...] + 1, 0).astype(F32)
    tag = jnp.concatenate([tag] * (EMB // SLOTS), axis=1)
    unit[SLOTS:UNIT, :] = jnp.broadcast_to(tag, (UNIT - SLOTS, EMB)).astype(BF16)


def slots_kernel(owner_row, owner_col, local_col, tags, rank_row):
    row, col = owner_row[...], owner_col[...]
    same = row == col
    up, across = iota((ROWS, ROWS), 0), iota((ROWS, ROWS), 1)
    ranks = jnp.sum(jnp.where(same & (up < across), 1, 0), axis=0, keepdims=True)
    ranks_col = jnp.sum(jnp.where(same & (across < up), 1, 0), axis=1, keepdims=True)
    rank_row[...] = ranks
    lane = iota((ROWS, CHUNK), 1)
    tags[...] = jnp.where(lane == ranks_col, local_col[...] + 1, 0).astype(F32).astype(BF16)


def first_kernel(own, left, right, far_a, far_b, mine, pre, rest, docs, sem):
    c = lax.axis_index("core")
    copies, row = [], 0
    for i, part in enumerate((own, left, right, far_a, far_b)):
        rows = part.shape[0]
        copies.append(pltpu.make_async_copy(part, docs.at[row : row + rows, :], sem.at[i]))
        row += rows
    for copy in copies:
        copy.start()
    w = jnp.concatenate([mine[j, 0:HALF, :] for j in range(4)], axis=1)
    for copy in copies:
        copy.wait()
    lines = docs[:, pl.ds(pl.multiple_of(c * HALF, HALF), HALF)]
    pre[...] = jnp.dot(lines, w, preferred_element_type=F32)
    rest[...] = docs[:, pl.ds(pl.multiple_of((1 - c) * HALF, HALF), HALF)]


def head_kernel(pre, rest, mine, other, out):
    x = lax.axis_index("x")
    w = jnp.concatenate([other[j, 0:HALF, :] for j in range(4)], axis=1)
    total = pre[...] + jnp.dot(rest[...], w, preferred_element_type=F32)
    hidden = jax.nn.gelu(total).astype(BF16)
    for k, weights in enumerate((mine, other)):
        rows = []
        for j in range(4):
            cut = [HALF + i * BLOCK for i in range(3)]
            rows.append(jnp.concatenate([weights[j, r : r + BLOCK, :] for r in cut], axis=1))
        total = jnp.dot(hidden, jnp.concatenate(rows, axis=0), preferred_element_type=F32)
        cut = slice(k * 3 * BLOCK, (k + 1) * 3 * BLOCK)
        for j, step in enumerate((0, 3, 1, 2)):
            out[lax.rem(x + step, 4), :, cut] = total[j * ROWS : (j + 1) * ROWS].astype(BF16)


def query_kernel(partial, owner_row, rank_row, tags, out):
    line = iota((OWNERS * LINES, ROWS), 0)
    inner = jnp.where(owner_row[...] == line // LINES, line % LINES, -1)
    place = [
        jnp.where(inner == (k * CAP + rank_row[...] if k < 3 else LINES - 1), 1.0, 0.0).astype(BF16)
        for k in range(4)
    ]
    proj = partial[0].astype(F32)
    for j in range(1, 4):
        proj = proj + partial[j].astype(F32)
    norm = jnp.sum(proj * proj, axis=1, keepdims=True)
    query = proj * (1.0 / jnp.sqrt(norm + EPS))
    low, high = query[:, 0 : EMB // 2], query[:, EMB // 2 :]
    straight = lax.axis_index("core") == 0
    query = jnp.concatenate(
        [jnp.where(straight, low, high), jnp.where(straight, high, low)], axis=1
    ).astype(BF16)
    total = jnp.dot(place[3], tags[...], preferred_element_type=F32)
    for k in range(3):
        total = total + jnp.dot(
            place[k], query[:, k * CHUNK : (k + 1) * CHUNK], preferred_element_type=F32
        )
    out[...] = total.astype(BF16).reshape(OWNERS, LINES, CHUNK)


def join_kernel(low, high, out):
    rows = low.shape[0]
    out[0:rows, :] = low[...]
    out[rows:, :] = high[...]


def score_kernel(arrived, own, left, right, top, bottom, out, held, sem):
    copy = pltpu.make_async_copy(bottom, held, sem.at[0])
    copy.start()
    parts = (own, left, right, top, held)
    row = iota((4 * OWNERS * CAP, 1), 0)
    kind, slot = row // (OWNERS * CAP), row % (OWNERS * CAP)
    line = jnp.where(kind < 3, kind * CAP + slot // OWNERS, LINES - 1)
    target = slot % OWNERS * LINES + line
    pick = jnp.where(iota((4 * OWNERS * CAP, OWNERS * LINES), 1) == target, 1.0, 0.0).astype(BF16)
    flat = arrived[...].reshape(OWNERS * LINES, CHUNK)
    moved = jnp.dot(pick, flat, preferred_element_type=F32)
    count = OWNERS * CAP
    query = jnp.concatenate(
        [moved[k * count : (k + 1) * count].astype(BF16) for k in range(3)], axis=1
    )
    slot = iota((count, CHUNK), 0) // OWNERS
    tag = jnp.sum(
        jnp.where(iota((count, CHUNK), 1) == slot, moved[3 * count :], 0.0), axis=1, keepdims=True
    )
    best = jnp.full((count, 2 * SLOTS), -1.0, F32)
    where = [(part, i * UNIT) for part in parts for i in range(part.shape[0] // UNIT)]
    for j in range(0, 16, 2):
        if j == 14:
            copy.wait()
        blocks, marks = [], []
        for part, row in where[j : j + 2]:
            blocks.append(part[row : row + SLOTS, :])
            marks.append(part[row + SLOTS : row + UNIT, 0:SLOTS].astype(F32)[0:1])
        scores = lax.dot_general(
            query,
            jnp.concatenate(blocks, axis=0),
            (((1,), (1,)), ((), ())),
            preferred_element_type=F32,
        )
        allowed = jnp.concatenate(marks, axis=1) == tag
        best = jnp.maximum(best, jnp.where(allowed, scores, -1.0))
    best = jnp.max(best, axis=1, keepdims=True)
    lane = iota((OWNERS, SLOTS), 1)
    result = jnp.zeros((OWNERS, SLOTS), F32)
    for s in range(CAP):
        result = jnp.where(lane == s, best[s * OWNERS : (s + 1) * OWNERS], result)
    out[...] = result


def answer_kernel(answers, owner_row, rank_row, out):
    mine = owner_row[...] == iota((OWNERS, ROWS), 0)
    total = jnp.zeros((1, ROWS), F32)
    for s in range(CAP):
        value = jnp.sum(jnp.where(mine, answers[:, s : s + 1], 0.0), axis=0, keepdims=True)
        total = jnp.where(rank_row[...] == s, value, total)
    out[...] = total


def shift(value, axis, step):
    return lax.ppermute(value, axis, [(i, (i + step) % 4) for i in range(4)])


def turn(value, move, turned):
    pairs = []
    for c in range(2):
        for y in range(4):
            for x in range(4):
                to = (y, move(x)) if (c == 1) == turned else (move(y), x)
                pairs.append((c * 16 + y * 4 + x, c * 16 + to[0] * 4 + to[1]))
    return lax.ppermute(value, ("core", "y", "x"), pairs)


def up(place):
    return (place + 1) % 4


def down(place):
    return (place + 3) % 4


HBM = pl.BlockSpec(memory_space=pltpu.HBM)
VMEM = pl.BlockSpec(memory_space=pltpu.VMEM)


def halved(*arrays):
    return pl.pallas_call(
        weights_kernel,
        out_shape=pltpu.VMEM((4, PACK, BLOCK), BF16),
        in_specs=[HBM] * 2,
        out_specs=VMEM,
        scratch_shapes=[
            pltpu.VMEM((HALF, BLOCK), BF16),
            pltpu.VMEM((BLOCK, 3 * BLOCK), BF16),
            pltpu.SemaphoreType.DMA((2,)),
        ],
        name="weights",
        compiler_params=PARAMS,
    )(*map(stay, arrays))


def normalised(*arrays):
    return pl.pallas_call(
        unit_kernel,
        out_shape=sds((UNIT, EMB), BF16),
        in_specs=[HBM] * 3,
        out_specs=VMEM,
        scratch_shapes=[
            pltpu.VMEM((SLOTS, EMB), BF16),
            pltpu.VMEM((1, SLOTS), I32),
            pltpu.VMEM((1, SLOTS), I32),
            pltpu.SemaphoreType.DMA((3,)),
        ],
        name="unit",
        compiler_params=PARAMS,
    )(*map(stay, arrays))


def first(*arrays):
    return pl.pallas_call(
        first_kernel,
        out_shape=(pltpu.VMEM((4 * ROWS, 4 * BLOCK), F32), pltpu.VMEM((4 * ROWS, HALF), BF16)),
        in_specs=[HBM] * 5 + [VMEM],
        out_specs=(VMEM, VMEM),
        scratch_shapes=[pltpu.VMEM((4 * ROWS, HID), BF16), pltpu.SemaphoreType.DMA((5,))],
        name="first",
        compiler_params=PARAMS,
    )(*arrays)


def joined(blocks, *parts):
    return call(join_kernel, sds((blocks * UNIT, EMB), BF16), "join")(*map(near, parts))


def near(value):
    return pltpu.with_memory_space_constraint(value, pltpu.VMEM)


def score(*arrays):
    return pl.pallas_call(
        score_kernel,
        out_shape=sds((OWNERS, SLOTS), F32),
        in_specs=[VMEM] * 5 + [HBM],
        out_specs=VMEM,
        scratch_shapes=[pltpu.VMEM((2 * UNIT, EMB), BF16), pltpu.SemaphoreType.DMA((1,))],
        name="score",
        compiler_params=PARAMS,
    )(*arrays)


def stay(value):
    return pltpu.with_memory_space_constraint(value, pltpu.HBM)


def swap(value):
    return lax.ppermute(value, "core", [(0, 1), (1, 0)])


def body(features, w_hidden, w_embed, members, doc_owner, doc_local, member_cluster, member_valid):
    dp = ("z", "core")
    mine = lax.all_to_all(near(halved(w_hidden, w_embed)), "y", 0, 0, tiled=True)
    docs = [shift(features, "x", 1), shift(features, "x", -1)]
    unit = normalised(members, member_cluster, member_valid)
    beside = turn(unit, lambda place: place ^ 1, False)
    cut = 48
    docs += [shift(docs[0][:cut], "x", 1), shift(docs[1][cut:], "x", -1)]

    start = lax.axis_index(("y", "x")) * ROWS
    owner = lax.dynamic_slice_in_dim(doc_owner[:, 0], start, ROWS, 0)
    local = lax.dynamic_slice_in_dim(doc_local, start, ROWS, 0)
    owner_row = owner.reshape(1, ROWS)
    tags, rank_row = call(
        slots_kernel,
        (
            sds((ROWS, CHUNK), BF16),
            sds((1, ROWS), I32),
        ),
        "slots",
    )(owner_row, owner.reshape(ROWS, 1), local.reshape(ROWS, 1))

    mine, tags, docs, beside = lax.optimization_barrier((mine, tags, docs, beside))
    pair = joined(2, unit, beside)
    opposite = turn(pair, lambda place: 3 - place, False)
    other = swap(mine)
    column = joined(4, pair, opposite)
    left, right = turn(column, up, True), turn(column, down, True)
    top, bottom = turn(left[: 2 * UNIT], up, True), turn(right[2 * UNIT :], down, True)
    columns = [column, left, right, top, bottom]
    pre, rest = first(*map(stay, (features, *docs)), mine)
    partial = call(head_kernel, pltpu.VMEM((4, ROWS, EMB), BF16), "head")(near(pre), near(rest), mine, other)
    partial = lax.all_to_all(near(partial), "x", 0, 0, tiled=True)
    outgoing = call(query_kernel, pltpu.VMEM((OWNERS, LINES, CHUNK), BF16), "query")(
        partial, owner_row, rank_row, tags
    )
    arrived = lax.all_to_all(near(outgoing), dp, 0, 0, tiled=True)
    best = score(arrived, *map(near, columns[:4]), stay(columns[4]))
    answers = lax.all_to_all(best, dp, 0, 0, tiled=True)
    result = call(answer_kernel, sds((1, ROWS), F32), "answer")(answers, owner_row, rank_row)
    return result.reshape(ROWS)


def solution(mesh):
    grid = Mesh(mesh.devices.reshape(16, 2, 4, 4), ("z", "core", "y", "x"))
    dp, tensor = ("z", "core"), ("y", "x")
    every = dp + tensor
    return jax.shard_map(
        body,
        mesh=grid,
        in_specs=(
            P(every, None),
            P(None, tensor),
            P(tensor, None),
            P(dp, tensor, None),
            P(dp, None),
            P(dp),
            P(dp, tensor),
            P(dp, tensor),
        ),
        out_specs=P(every),
        check_vma=False,
    )
```

```python
import jax
import jax.numpy as jnp
import numpy as np
from jax import lax
from jax.experimental import pallas as pl
from jax.experimental.pallas import tpu as pltpu
from jax.sharding import Mesh, PartitionSpec as P

EPS = 1e-06
HID, EMB, ROWS, SLOTS, BLOCK, OWNERS, CAP = 2048, 768, 80, 128, 128, 32, 5
HALF = HID // 2
PACK = HALF + 3 * BLOCK
CHUNK = 256
LINES = 16
UNIT = SLOTS + 16
F32, BF16, I32 = jnp.float32, jnp.bfloat16, jnp.int32
PARAMS = pltpu.CompilerParams(vmem_limit_bytes=16 << 20)


def sds(shape, dtype):
    return jax.ShapeDtypeStruct(shape, dtype)


def iota(shape, dim):
    return lax.broadcasted_iota(I32, shape, dim)


def call(body, out, name):
    vm = pl.BlockSpec(memory_space=pltpu.VMEM)

    def run(*args):
        specs = [vm] * len(args)
        outs = jax.tree.map(lambda _: vm, out)
        return pl.pallas_call(
            body, out_shape=out, in_specs=specs, out_specs=outs, name=name, compiler_params=PARAMS
        )(*args)

    return run


def weights_kernel(w_hidden, w_embed, half, upper, lower, sem):
    c = lax.axis_index("core")
    copies = [
        pltpu.make_async_copy(
            w_hidden.at[pl.ds(pl.multiple_of(c * HALF, HALF), HALF), :], upper, sem.at[0]
        ),
        pltpu.make_async_copy(
            w_embed.at[:, pl.ds(pl.multiple_of(c * 3 * BLOCK, BLOCK), 3 * BLOCK)], lower, sem.at[1]
        ),
    ]
    for copy in copies:
        copy.start()
    for copy in copies:
        copy.wait()
    for j in range(4):
        half[j, 0:HALF, :] = upper[...]
        for i in range(3):
            half[j, HALF + i * BLOCK : HALF + (i + 1) * BLOCK, :] = lower[
                :, i * BLOCK : (i + 1) * BLOCK
            ]


def unit_kernel(members, cluster, valid, unit, held, slots, live, sem):
    copies = [
        pltpu.make_async_copy(members.at[0], held, sem.at[0]),
        pltpu.make_async_copy(cluster, slots, sem.at[1]),
        pltpu.make_async_copy(valid, live, sem.at[2]),
    ]
    for copy in copies:
        copy.start()
    for copy in copies:
        copy.wait()
    values = held[...].astype(F32)
    norm = jnp.sum(values * values, axis=1, keepdims=True)
    unit[0:SLOTS, :] = (values * (1.0 / jnp.sqrt(norm + EPS))).astype(BF16)
    tag = jnp.where(live[...] == 1, slots[...] + 1, 0).astype(F32)
    tag = jnp.concatenate([tag] * (EMB // SLOTS), axis=1)
    unit[SLOTS:UNIT, :] = jnp.broadcast_to(tag, (UNIT - SLOTS, EMB)).astype(BF16)


def slots_kernel(owner_row, owner_col, local_col, tags, rank_row):
    row, col = owner_row[...], owner_col[...]
    same = row == col
    up, across = iota((ROWS, ROWS), 0), iota((ROWS, ROWS), 1)
    ranks = jnp.sum(jnp.where(same & (up < across), 1, 0), axis=0, keepdims=True)
    ranks_col = jnp.sum(jnp.where(same & (across < up), 1, 0), axis=1, keepdims=True)
    rank_row[...] = ranks
    lane = iota((ROWS, CHUNK), 1)
    tags[...] = jnp.where(lane == ranks_col, local_col[...] + 1, 0).astype(F32).astype(BF16)


def first_kernel(own, left, right, far_a, far_b, mine, pre, rest, docs, sem):
    c = lax.axis_index("core")
    copies, row = [], 0
    for i, part in enumerate((own, left, right, far_a, far_b)):
        rows = part.shape[0]
        copies.append(pltpu.make_async_copy(part, docs.at[row : row + rows, :], sem.at[i]))
        row += rows
    for copy in copies:
        copy.start()
    w = jnp.concatenate([mine[j, 0:HALF, :] for j in range(4)], axis=1)
    for copy in copies:
        copy.wait()
    lines = docs[:, pl.ds(pl.multiple_of(c * HALF, HALF), HALF)]
    pre[...] = jnp.dot(lines, w, preferred_element_type=F32)
    rest[...] = docs[:, pl.ds(pl.multiple_of((1 - c) * HALF, HALF), HALF)]


def head_kernel(pre, rest, mine, other, out):
    x = lax.axis_index("x")
    w = jnp.concatenate([other[j, 0:HALF, :] for j in range(4)], axis=1)
    total = pre[...] + jnp.dot(rest[...], w, preferred_element_type=F32)
    hidden = jax.nn.gelu(total).astype(BF16)
    for k, weights in enumerate((mine, other)):
        rows = []
        for j in range(4):
            cut = [HALF + i * BLOCK for i in range(3)]
            rows.append(jnp.concatenate([weights[j, r : r + BLOCK, :] for r in cut], axis=1))
        total = jnp.dot(hidden, jnp.concatenate(rows, axis=0), preferred_element_type=F32)
        cut = slice(k * 3 * BLOCK, (k + 1) * 3 * BLOCK)
        for j, step in enumerate((0, 3, 1, 2)):
            out[lax.rem(x + step, 4), :, cut] = total[j * ROWS : (j + 1) * ROWS].astype(BF16)


def query_kernel(partial, owner_row, rank_row, tags, out):
    line = iota((OWNERS * LINES, ROWS), 0)
    inner = jnp.where(owner_row[...] == line // LINES, line % LINES, -1)
    place = [
        jnp.where(inner == (k * CAP + rank_row[...] if k < 3 else LINES - 1), 1.0, 0.0).astype(BF16)
        for k in range(4)
    ]
    proj = partial[0].astype(F32)
    for j in range(1, 4):
        proj = proj + partial[j].astype(F32)
    norm = jnp.sum(proj * proj, axis=1, keepdims=True)
    query = proj * (1.0 / jnp.sqrt(norm + EPS))
    low, high = query[:, 0 : EMB // 2], query[:, EMB // 2 :]
    straight = lax.axis_index("core") == 0
    query = jnp.concatenate(
        [jnp.where(straight, low, high), jnp.where(straight, high, low)], axis=1
    ).astype(BF16)
    total = jnp.dot(place[3], tags[...], preferred_element_type=F32)
    for k in range(3):
        total = total + jnp.dot(
            place[k], query[:, k * CHUNK : (k + 1) * CHUNK], preferred_element_type=F32
        )
    out[...] = total.astype(BF16).reshape(OWNERS, LINES, CHUNK)


def join_kernel(low, high, out):
    rows = low.shape[0]
    out[0:rows, :] = low[...]
    out[rows:, :] = high[...]


def score_kernel(arrived, own, left, right, top, bottom, out, held, sem):
    copy = pltpu.make_async_copy(bottom, held, sem.at[0])
    copy.start()
    parts = (own, left, right, top, held)
    row = iota((4 * OWNERS * CAP, 1), 0)
    kind, slot = row // (OWNERS * CAP), row % (OWNERS * CAP)
    line = jnp.where(kind < 3, kind * CAP + slot // OWNERS, LINES - 1)
    target = slot % OWNERS * LINES + line
    pick = jnp.where(iota((4 * OWNERS * CAP, OWNERS * LINES), 1) == target, 1.0, 0.0).astype(BF16)
    flat = arrived[...].reshape(OWNERS * LINES, CHUNK)
    moved = jnp.dot(pick, flat, preferred_element_type=F32)
    count = OWNERS * CAP
    query = jnp.concatenate(
        [moved[k * count : (k + 1) * count].astype(BF16) for k in range(3)], axis=1
    )
    slot = iota((count, CHUNK), 0) // OWNERS
    tag = jnp.sum(
        jnp.where(iota((count, CHUNK), 1) == slot, moved[3 * count :], 0.0), axis=1, keepdims=True
    )
    best = jnp.full((count, 2 * SLOTS), -1.0, F32)
    where = [(part, i * UNIT) for part in parts for i in range(part.shape[0] // UNIT)]
    for j in range(0, 16, 2):
        if j == 14:
            copy.wait()
        blocks, marks = [], []
        for part, row in where[j : j + 2]:
            blocks.append(part[row : row + SLOTS, :])
            marks.append(part[row + SLOTS : row + UNIT, 0:SLOTS].astype(F32)[0:1])
        scores = lax.dot_general(
            query,
            jnp.concatenate(blocks, axis=0),
            (((1,), (1,)), ((), ())),
            preferred_element_type=F32,
        )
        allowed = jnp.concatenate(marks, axis=1) == tag
        best = jnp.maximum(best, jnp.where(allowed, scores, -1.0))
    best = jnp.max(best, axis=1, keepdims=True)
    lane = iota((OWNERS, SLOTS), 1)
    result = jnp.zeros((OWNERS, SLOTS), F32)
    for s in range(CAP):
        result = jnp.where(lane == s, best[s * OWNERS : (s + 1) * OWNERS], result)
    out[...] = result


def answer_kernel(answers, owner_row, rank_row, out):
    mine = owner_row[...] == iota((OWNERS, ROWS), 0)
    total = jnp.zeros((1, ROWS), F32)
    for s in range(CAP):
        value = jnp.sum(jnp.where(mine, answers[:, s : s + 1], 0.0), axis=0, keepdims=True)
        total = jnp.where(rank_row[...] == s, value, total)
    out[...] = total


def shift(value, axis, step):
    return lax.ppermute(value, axis, [(i, (i + step) % 4) for i in range(4)])


def turn(value, move, turned):
    pairs = []
    for c in range(2):
        for y in range(4):
            for x in range(4):
                to = (y, move(x)) if (c == 1) == turned else (move(y), x)
                pairs.append((c * 16 + y * 4 + x, c * 16 + to[0] * 4 + to[1]))
    return lax.ppermute(value, ("core", "y", "x"), pairs)


def up(place):
    return (place + 1) % 4


def down(place):
    return (place + 3) % 4


HBM = pl.BlockSpec(memory_space=pltpu.HBM)
VMEM = pl.BlockSpec(memory_space=pltpu.VMEM)


def halved(*arrays):
    return pl.pallas_call(
        weights_kernel,
        out_shape=pltpu.VMEM((4, PACK, BLOCK), BF16),
        in_specs=[HBM] * 2,
        out_specs=VMEM,
        scratch_shapes=[
            pltpu.VMEM((HALF, BLOCK), BF16),
            pltpu.VMEM((BLOCK, 3 * BLOCK), BF16),
            pltpu.SemaphoreType.DMA((2,)),
        ],
        name="weights",
        compiler_params=PARAMS,
    )(*map(stay, arrays))


def normalised(*arrays):
    return pl.pallas_call(
        unit_kernel,
        out_shape=sds((UNIT, EMB), BF16),
        in_specs=[HBM] * 3,
        out_specs=VMEM,
        scratch_shapes=[
            pltpu.VMEM((SLOTS, EMB), BF16),
            pltpu.VMEM((1, SLOTS), I32),
            pltpu.VMEM((1, SLOTS), I32),
            pltpu.SemaphoreType.DMA((3,)),
        ],
        name="unit",
        compiler_params=PARAMS,
    )(*map(stay, arrays))


def first(*arrays):
    return pl.pallas_call(
        first_kernel,
        out_shape=(pltpu.VMEM((4 * ROWS, 4 * BLOCK), F32), pltpu.VMEM((4 * ROWS, HALF), BF16)),
        in_specs=[HBM] * 5 + [VMEM],
        out_specs=(VMEM, VMEM),
        scratch_shapes=[pltpu.VMEM((4 * ROWS, HID), BF16), pltpu.SemaphoreType.DMA((5,))],
        name="first",
        cost_estimate=pl.CostEstimate(flops=30 << 30, bytes_accessed=4 << 20, transcendentals=0),
        compiler_params=PARAMS,
    )(*arrays)


def joined(blocks, *parts):
    return call(join_kernel, sds((blocks * UNIT, EMB), BF16), "join")(*map(near, parts))


def near(value):
    return pltpu.with_memory_space_constraint(value, pltpu.VMEM)


def score(*arrays):
    return pl.pallas_call(
        score_kernel,
        out_shape=sds((OWNERS, SLOTS), F32),
        in_specs=[VMEM] * 5 + [HBM],
        out_specs=VMEM,
        scratch_shapes=[pltpu.VMEM((2 * UNIT, EMB), BF16), pltpu.SemaphoreType.DMA((1,))],
        name="score",
        compiler_params=PARAMS,
    )(*arrays)


def stay(value):
    return pltpu.with_memory_space_constraint(value, pltpu.HBM)


def swap(value):
    return lax.ppermute(value, "core", [(0, 1), (1, 0)])


def body(features, w_hidden, w_embed, members, doc_owner, doc_local, member_cluster, member_valid):
    dp = ("z", "core")
    mine = lax.all_to_all(near(halved(w_hidden, w_embed)), "y", 0, 0, tiled=True)
    docs = [shift(features, "x", 1), shift(features, "x", -1)]
    unit = normalised(members, member_cluster, member_valid)
    beside = turn(unit, lambda place: place ^ 1, False)
    cut = 48
    docs += [shift(docs[0][:cut], "x", 1), shift(docs[1][cut:], "x", -1)]

    start = lax.axis_index(("y", "x")) * ROWS
    owner = lax.dynamic_slice_in_dim(doc_owner[:, 0], start, ROWS, 0)
    local = lax.dynamic_slice_in_dim(doc_local, start, ROWS, 0)
    owner_row = owner.reshape(1, ROWS)
    tags, rank_row = call(
        slots_kernel,
        (
            sds((ROWS, CHUNK), BF16),
            sds((1, ROWS), I32),
        ),
        "slots",
    )(owner_row, owner.reshape(ROWS, 1), local.reshape(ROWS, 1))

    mine, tags, docs[:2], beside = lax.optimization_barrier((mine, tags, docs[:2], beside))
    pair = joined(2, unit, beside)
    opposite = turn(pair, lambda place: 3 - place, False)
    other = swap(mine)
    column = joined(4, pair, opposite)
    left, right = turn(column, up, True), turn(column, down, True)
    top, bottom = turn(left[: 2 * UNIT], up, True), turn(right[2 * UNIT :], down, True)
    columns = [column, left, right, top, bottom]
    pre, rest = first(*map(stay, (features, *docs)), mine)
    partial = call(head_kernel, pltpu.VMEM((4, ROWS, EMB), BF16), "head")(near(pre), near(rest), mine, other)
    partial = lax.all_to_all(near(partial), "x", 0, 0, tiled=True)
    outgoing = call(query_kernel, pltpu.VMEM((OWNERS, LINES, CHUNK), BF16), "query")(
        partial, owner_row, rank_row, tags
    )
    arrived = lax.all_to_all(near(outgoing), dp, 0, 0, tiled=True)
    best = score(arrived, *map(near, columns[:4]), stay(columns[4]))
    answers = lax.all_to_all(best, dp, 0, 0, tiled=True)
    result = call(answer_kernel, sds((1, ROWS), F32), "answer")(answers, owner_row, rank_row)
    return result.reshape(ROWS)


def solution(mesh):
    grid = Mesh(mesh.devices.reshape(16, 2, 4, 4), ("z", "core", "y", "x"))
    dp, tensor = ("z", "core"), ("y", "x")
    every = dp + tensor
    return jax.shard_map(
        body,
        mesh=grid,
        in_specs=(
            P(every, None),
            P(None, tensor),
            P(tensor, None),
            P(dp, tensor, None),
            P(dp, None),
            P(dp),
            P(dp, tensor),
            P(dp, tensor),
        ),
        out_specs=P(every),
        check_vma=False,
    )
```

```python
import jax
import jax.numpy as jnp
import numpy as np
from jax import lax
from jax.experimental import pallas as pl
from jax.experimental.pallas import tpu as pltpu
from jax.sharding import Mesh, PartitionSpec as P

EPS = 1e-06
HID, EMB, ROWS, SLOTS, BLOCK, OWNERS, CAP = 2048, 768, 80, 128, 128, 32, 5
HALF = HID // 2
PACK = HALF + 3 * BLOCK
CHUNK = 256
LINES = 16
UNIT = SLOTS + 16
F32, BF16, I32 = jnp.float32, jnp.bfloat16, jnp.int32
PARAMS = pltpu.CompilerParams(vmem_limit_bytes=16 << 20)


def sds(shape, dtype):
    return jax.ShapeDtypeStruct(shape, dtype)


def iota(shape, dim):
    return lax.broadcasted_iota(I32, shape, dim)


def call(body, out, name):
    vm = pl.BlockSpec(memory_space=pltpu.VMEM)

    def run(*args):
        specs = [vm] * len(args)
        outs = jax.tree.map(lambda _: vm, out)
        return pl.pallas_call(
            body, out_shape=out, in_specs=specs, out_specs=outs, name=name, compiler_params=PARAMS
        )(*args)

    return run


def weights_kernel(w_hidden, w_embed, half, upper, lower, sem):
    c = lax.axis_index("core")
    copies = [
        pltpu.make_async_copy(
            w_hidden.at[pl.ds(pl.multiple_of(c * HALF, HALF), HALF), :], upper, sem.at[0]
        ),
        pltpu.make_async_copy(
            w_embed.at[:, pl.ds(pl.multiple_of(c * 3 * BLOCK, BLOCK), 3 * BLOCK)], lower, sem.at[1]
        ),
    ]
    for copy in copies:
        copy.start()
    for copy in copies:
        copy.wait()
    for j in range(4):
        half[j, 0:HALF, :] = upper[...]
        for i in range(3):
            half[j, HALF + i * BLOCK : HALF + (i + 1) * BLOCK, :] = lower[
                :, i * BLOCK : (i + 1) * BLOCK
            ]


def unit_kernel(members, cluster, valid, unit, held, slots, live, sem):
    copies = [
        pltpu.make_async_copy(members.at[0], held, sem.at[0]),
        pltpu.make_async_copy(cluster, slots, sem.at[1]),
        pltpu.make_async_copy(valid, live, sem.at[2]),
    ]
    for copy in copies:
        copy.start()
    for copy in copies:
        copy.wait()
    values = held[...].astype(F32)
    norm = jnp.sum(values * values, axis=1, keepdims=True)
    unit[0:SLOTS, :] = (values * (1.0 / jnp.sqrt(norm + EPS))).astype(BF16)
    tag = jnp.where(live[...] == 1, slots[...] + 1, 0).astype(F32)
    tag = jnp.concatenate([tag] * (EMB // SLOTS), axis=1)
    unit[SLOTS:UNIT, :] = jnp.broadcast_to(tag, (UNIT - SLOTS, EMB)).astype(BF16)


def slots_kernel(owner_row, owner_col, local_col, tags, rank_row):
    row, col = owner_row[...], owner_col[...]
    same = row == col
    up, across = iota((ROWS, ROWS), 0), iota((ROWS, ROWS), 1)
    ranks = jnp.sum(jnp.where(same & (up < across), 1, 0), axis=0, keepdims=True)
    ranks_col = jnp.sum(jnp.where(same & (across < up), 1, 0), axis=1, keepdims=True)
    rank_row[...] = ranks
    lane = iota((ROWS, CHUNK), 1)
    tags[...] = jnp.where(lane == ranks_col, local_col[...] + 1, 0).astype(F32).astype(BF16)


def first_kernel(own, left, right, far_a, far_b, mine, pre, rest, docs, sem):
    c = lax.axis_index("core")
    copies, row = [], 0
    for i, part in enumerate((own, left, right)):
        rows = part.shape[0]
        copies.append(pltpu.make_async_copy(part, docs.at[row : row + rows, :], sem.at[i]))
        row += rows
    for copy in copies:
        copy.start()
    for part in (far_a, far_b):
        docs[row : row + part.shape[0], :] = part[...]
        row += part.shape[0]
    w = jnp.concatenate([mine[j, 0:HALF, :] for j in range(4)], axis=1)
    for copy in copies:
        copy.wait()
    lines = docs[:, pl.ds(pl.multiple_of(c * HALF, HALF), HALF)]
    pre[...] = jnp.dot(lines, w, preferred_element_type=F32)
    rest[...] = docs[:, pl.ds(pl.multiple_of((1 - c) * HALF, HALF), HALF)]


def head_kernel(pre, rest, mine, other, out):
    x = lax.axis_index("x")
    w = jnp.concatenate([other[j, 0:HALF, :] for j in range(4)], axis=1)
    total = pre[...] + jnp.dot(rest[...], w, preferred_element_type=F32)
    hidden = jax.nn.gelu(total).astype(BF16)
    for k, weights in enumerate((mine, other)):
        rows = []
        for j in range(4):
            cut = [HALF + i * BLOCK for i in range(3)]
            rows.append(jnp.concatenate([weights[j, r : r + BLOCK, :] for r in cut], axis=1))
        total = jnp.dot(hidden, jnp.concatenate(rows, axis=0), preferred_element_type=F32)
        cut = slice(k * 3 * BLOCK, (k + 1) * 3 * BLOCK)
        for j, step in enumerate((0, 3, 1, 2)):
            out[lax.rem(x + step, 4), :, cut] = total[j * ROWS : (j + 1) * ROWS].astype(BF16)


def query_kernel(partial, owner_row, rank_row, tags, out):
    line = iota((OWNERS * LINES, ROWS), 0)
    inner = jnp.where(owner_row[...] == line // LINES, line % LINES, -1)
    place = [
        jnp.where(inner == (k * CAP + rank_row[...] if k < 3 else LINES - 1), 1.0, 0.0).astype(BF16)
        for k in range(4)
    ]
    proj = partial[0].astype(F32)
    for j in range(1, 4):
        proj = proj + partial[j].astype(F32)
    norm = jnp.sum(proj * proj, axis=1, keepdims=True)
    query = proj * (1.0 / jnp.sqrt(norm + EPS))
    low, high = query[:, 0 : EMB // 2], query[:, EMB // 2 :]
    straight = lax.axis_index("core") == 0
    query = jnp.concatenate(
        [jnp.where(straight, low, high), jnp.where(straight, high, low)], axis=1
    ).astype(BF16)
    total = jnp.dot(place[3], tags[...], preferred_element_type=F32)
    for k in range(3):
        total = total + jnp.dot(
            place[k], query[:, k * CHUNK : (k + 1) * CHUNK], preferred_element_type=F32
        )
    out[...] = total.astype(BF16).reshape(OWNERS, LINES, CHUNK)


def join_kernel(low, high, out):
    rows = low.shape[0]
    out[0:rows, :] = low[...]
    out[rows:, :] = high[...]


def score_kernel(arrived, own, left, right, top, bottom, out, held, sem):
    copies = [
        pltpu.make_async_copy(top, held.at[0 : 2 * UNIT, :], sem.at[0]),
        pltpu.make_async_copy(bottom, held.at[2 * UNIT :, :], sem.at[1]),
    ]
    for copy in copies:
        copy.start()
    parts = (own, left, right, held)
    row = iota((4 * OWNERS * CAP, 1), 0)
    kind, slot = row // (OWNERS * CAP), row % (OWNERS * CAP)
    line = jnp.where(kind < 3, kind * CAP + slot // OWNERS, LINES - 1)
    target = slot % OWNERS * LINES + line
    pick = jnp.where(iota((4 * OWNERS * CAP, OWNERS * LINES), 1) == target, 1.0, 0.0).astype(BF16)
    flat = arrived[...].reshape(OWNERS * LINES, CHUNK)
    moved = jnp.dot(pick, flat, preferred_element_type=F32)
    count = OWNERS * CAP
    query = jnp.concatenate(
        [moved[k * count : (k + 1) * count].astype(BF16) for k in range(3)], axis=1
    )
    slot = iota((count, CHUNK), 0) // OWNERS
    tag = jnp.sum(
        jnp.where(iota((count, CHUNK), 1) == slot, moved[3 * count :], 0.0), axis=1, keepdims=True
    )
    best = jnp.full((count, 2 * SLOTS), -1.0, F32)
    where = [(part, i * UNIT) for part in parts for i in range(part.shape[0] // UNIT)]
    for j in range(0, 16, 2):
        if j == 12:
            for copy in copies:
                copy.wait()
        blocks, marks = [], []
        for part, row in where[j : j + 2]:
            blocks.append(part[row : row + SLOTS, :])
            marks.append(part[row + SLOTS : row + UNIT, 0:SLOTS].astype(F32)[0:1])
        scores = lax.dot_general(
            query,
            jnp.concatenate(blocks, axis=0),
            (((1,), (1,)), ((), ())),
            preferred_element_type=F32,
        )
        allowed = jnp.concatenate(marks, axis=1) == tag
        best = jnp.maximum(best, jnp.where(allowed, scores, -1.0))
    best = jnp.max(best, axis=1, keepdims=True)
    lane = iota((OWNERS, SLOTS), 1)
    result = jnp.zeros((OWNERS, SLOTS), F32)
    for s in range(CAP):
        result = jnp.where(lane == s, best[s * OWNERS : (s + 1) * OWNERS], result)
    out[...] = result


def answer_kernel(answers, owner_row, rank_row, out):
    mine = owner_row[...] == iota((OWNERS, ROWS), 0)
    total = jnp.zeros((1, ROWS), F32)
    for s in range(CAP):
        value = jnp.sum(jnp.where(mine, answers[:, s : s + 1], 0.0), axis=0, keepdims=True)
        total = jnp.where(rank_row[...] == s, value, total)
    out[...] = total


def shift(value, axis, step):
    return lax.ppermute(value, axis, [(i, (i + step) % 4) for i in range(4)])


def turn(value, move, turned):
    pairs = []
    for c in range(2):
        for y in range(4):
            for x in range(4):
                to = (y, move(x)) if (c == 1) == turned else (move(y), x)
                pairs.append((c * 16 + y * 4 + x, c * 16 + to[0] * 4 + to[1]))
    return lax.ppermute(value, ("core", "y", "x"), pairs)


def up(place):
    return (place + 1) % 4


def down(place):
    return (place + 3) % 4


HBM = pl.BlockSpec(memory_space=pltpu.HBM)
VMEM = pl.BlockSpec(memory_space=pltpu.VMEM)


def halved(*arrays):
    return pl.pallas_call(
        weights_kernel,
        out_shape=pltpu.VMEM((4, PACK, BLOCK), BF16),
        in_specs=[HBM] * 2,
        out_specs=VMEM,
        scratch_shapes=[
            pltpu.VMEM((HALF, BLOCK), BF16),
            pltpu.VMEM((BLOCK, 3 * BLOCK), BF16),
            pltpu.SemaphoreType.DMA((2,)),
        ],
        name="weights",
        compiler_params=PARAMS,
    )(*map(stay, arrays))


def normalised(*arrays):
    return pl.pallas_call(
        unit_kernel,
        out_shape=sds((UNIT, EMB), BF16),
        in_specs=[HBM] * 3,
        out_specs=VMEM,
        scratch_shapes=[
            pltpu.VMEM((SLOTS, EMB), BF16),
            pltpu.VMEM((1, SLOTS), I32),
            pltpu.VMEM((1, SLOTS), I32),
            pltpu.SemaphoreType.DMA((3,)),
        ],
        name="unit",
        compiler_params=PARAMS,
    )(*map(stay, arrays))


def first(*arrays):
    return pl.pallas_call(
        first_kernel,
        out_shape=(pltpu.VMEM((4 * ROWS, 4 * BLOCK), F32), pltpu.VMEM((4 * ROWS, HALF), BF16)),
        in_specs=[HBM] * 3 + [VMEM] * 3,
        out_specs=(VMEM, VMEM),
        scratch_shapes=[pltpu.VMEM((4 * ROWS, HID), BF16), pltpu.SemaphoreType.DMA((3,))],
        name="first",
        cost_estimate=pl.CostEstimate(flops=30 << 30, bytes_accessed=4 << 20, transcendentals=0),
        compiler_params=PARAMS,
    )(*arrays)


def joined(blocks, *parts):
    return call(join_kernel, sds((blocks * UNIT, EMB), BF16), "join")(*map(near, parts))


def near(value):
    return pltpu.with_memory_space_constraint(value, pltpu.VMEM)


def score(*arrays):
    return pl.pallas_call(
        score_kernel,
        out_shape=sds((OWNERS, SLOTS), F32),
        in_specs=[VMEM] * 4 + [HBM] * 2,
        out_specs=VMEM,
        scratch_shapes=[pltpu.VMEM((4 * UNIT, EMB), BF16), pltpu.SemaphoreType.DMA((2,))],
        name="score",
        compiler_params=PARAMS,
    )(*arrays)


def stay(value):
    return pltpu.with_memory_space_constraint(value, pltpu.HBM)


def swap(value):
    return lax.ppermute(value, "core", [(0, 1), (1, 0)])


def body(features, w_hidden, w_embed, members, doc_owner, doc_local, member_cluster, member_valid):
    dp = ("z", "core")
    mine = lax.all_to_all(near(halved(w_hidden, w_embed)), "y", 0, 0, tiled=True)
    docs = [shift(features, "x", 1), shift(features, "x", -1)]
    unit = normalised(members, member_cluster, member_valid)
    beside = turn(unit, lambda place: place ^ 1, False)
    cut = 48
    docs += [shift(docs[0][:cut], "x", 1), shift(docs[1][cut:], "x", -1)]

    start = lax.axis_index(("y", "x")) * ROWS
    owner = lax.dynamic_slice_in_dim(doc_owner[:, 0], start, ROWS, 0)
    local = lax.dynamic_slice_in_dim(doc_local, start, ROWS, 0)
    owner_row = owner.reshape(1, ROWS)
    tags, rank_row = call(
        slots_kernel,
        (
            sds((ROWS, CHUNK), BF16),
            sds((1, ROWS), I32),
        ),
        "slots",
    )(owner_row, owner.reshape(ROWS, 1), local.reshape(ROWS, 1))

    mine, tags, docs[:2], beside = lax.optimization_barrier((mine, tags, docs[:2], beside))
    pair = joined(2, unit, beside)
    opposite = turn(pair, lambda place: 3 - place, False)
    other = swap(mine)
    column = joined(4, pair, opposite)
    left, right = turn(column, up, True), turn(column, down, True)
    top, bottom = turn(left[: 2 * UNIT], up, True), turn(right[2 * UNIT :], down, True)
    columns = [column, left, right, top, bottom]
    pre, rest = first(*map(stay, (features, *docs[:2])), *map(near, docs[2:]), mine)
    partial = call(head_kernel, pltpu.VMEM((4, ROWS, EMB), BF16), "head")(near(pre), near(rest), mine, other)
    partial = lax.all_to_all(near(partial), "x", 0, 0, tiled=True)
    outgoing = call(query_kernel, pltpu.VMEM((OWNERS, LINES, CHUNK), BF16), "query")(
        partial, owner_row, rank_row, tags
    )
    arrived = lax.all_to_all(near(outgoing), dp, 0, 0, tiled=True)
    best = score(arrived, *map(near, columns[:3]), *map(stay, columns[3:]))
    answers = lax.all_to_all(best, dp, 0, 0, tiled=True)
    result = call(answer_kernel, sds((1, ROWS), F32), "answer")(answers, owner_row, rank_row)
    return result.reshape(ROWS)


def solution(mesh):
    grid = Mesh(mesh.devices.reshape(16, 2, 4, 4), ("z", "core", "y", "x"))
    dp, tensor = ("z", "core"), ("y", "x")
    every = dp + tensor
    return jax.shard_map(
        body,
        mesh=grid,
        in_specs=(
            P(every, None),
            P(None, tensor),
            P(tensor, None),
            P(dp, tensor, None),
            P(dp, None),
            P(dp),
            P(dp, tensor),
            P(dp, tensor),
        ),
        out_specs=P(every),
        check_vma=False,
    )
```

```python
import jax
import jax.numpy as jnp
import numpy as np
from jax import lax
from jax.experimental import pallas as pl
from jax.experimental.pallas import tpu as pltpu
from jax.sharding import Mesh, PartitionSpec as P

EPS = 1e-06
HID, EMB, ROWS, SLOTS, BLOCK, OWNERS, CAP = 2048, 768, 80, 128, 128, 32, 5
HALF = HID // 2
PACK = HALF + 3 * BLOCK
CHUNK = 256
LINES = 16
UNIT = SLOTS + 16
F32, BF16, I32 = jnp.float32, jnp.bfloat16, jnp.int32
PARAMS = pltpu.CompilerParams(vmem_limit_bytes=16 << 20)


def sds(shape, dtype):
    return jax.ShapeDtypeStruct(shape, dtype)


def iota(shape, dim):
    return lax.broadcasted_iota(I32, shape, dim)


def call(body, out, name):
    vm = pl.BlockSpec(memory_space=pltpu.VMEM)

    def run(*args):
        specs = [vm] * len(args)
        outs = jax.tree.map(lambda _: vm, out)
        return pl.pallas_call(
            body, out_shape=out, in_specs=specs, out_specs=outs, name=name, compiler_params=PARAMS
        )(*args)

    return run


def weights_kernel(w_hidden, w_embed, half, upper, lower, sem):
    c = lax.axis_index("core")
    copies = [
        pltpu.make_async_copy(
            w_hidden.at[pl.ds(pl.multiple_of(c * HALF, HALF), HALF), :], upper, sem.at[0]
        ),
        pltpu.make_async_copy(
            w_embed.at[:, pl.ds(pl.multiple_of(c * 3 * BLOCK, BLOCK), 3 * BLOCK)], lower, sem.at[1]
        ),
    ]
    for copy in copies:
        copy.start()
    for copy in copies:
        copy.wait()
    for j in range(4):
        half[j, 0:HALF, :] = upper[...]
        for i in range(3):
            half[j, HALF + i * BLOCK : HALF + (i + 1) * BLOCK, :] = lower[
                :, i * BLOCK : (i + 1) * BLOCK
            ]


def unit_kernel(members, cluster, valid, unit, held, slots, live, sem):
    copies = [
        pltpu.make_async_copy(members.at[0], held, sem.at[0]),
        pltpu.make_async_copy(cluster, slots, sem.at[1]),
        pltpu.make_async_copy(valid, live, sem.at[2]),
    ]
    for copy in copies:
        copy.start()
    for copy in copies:
        copy.wait()
    values = held[...].astype(F32)
    norm = jnp.sum(values * values, axis=1, keepdims=True)
    unit[0:SLOTS, :] = (values * (1.0 / jnp.sqrt(norm + EPS))).astype(BF16)
    tag = jnp.where(live[...] == 1, slots[...] + 1, 0).astype(F32)
    tag = jnp.concatenate([tag] * (EMB // SLOTS), axis=1)
    unit[SLOTS:UNIT, :] = jnp.broadcast_to(tag, (UNIT - SLOTS, EMB)).astype(BF16)


def slots_kernel(owner_row, owner_col, local_col, tags, rank_row):
    row, col = owner_row[...], owner_col[...]
    same = row == col
    up, across = iota((ROWS, ROWS), 0), iota((ROWS, ROWS), 1)
    ranks = jnp.sum(jnp.where(same & (up < across), 1, 0), axis=0, keepdims=True)
    ranks_col = jnp.sum(jnp.where(same & (across < up), 1, 0), axis=1, keepdims=True)
    rank_row[...] = ranks
    lane = iota((ROWS, CHUNK), 1)
    tags[...] = jnp.where(lane == ranks_col, local_col[...] + 1, 0).astype(F32).astype(BF16)


def first_kernel(own, left, right, far_a, far_b, mine, pre, rest, docs, sem):
    c = lax.axis_index("core")
    copies, row = [], 0
    for i, part in enumerate((own, left, right)):
        rows = part.shape[0]
        copies.append(pltpu.make_async_copy(part, docs.at[row : row + rows, :], sem.at[i]))
        row += rows
    for copy in copies:
        copy.start()
    for part in (far_a, far_b):
        docs[row : row + part.shape[0], :] = part[...]
        row += part.shape[0]
    w = jnp.concatenate([mine[j, 0:HALF, :] for j in range(4)], axis=1)
    for copy in copies:
        copy.wait()
    lines = docs[:, pl.ds(pl.multiple_of(c * HALF, HALF), HALF)]
    pre[...] = jnp.dot(lines, w, preferred_element_type=F32)
    rest[...] = docs[:, pl.ds(pl.multiple_of((1 - c) * HALF, HALF), HALF)]


def head_kernel(pre, rest, mine, other, out):
    x = lax.axis_index("x")
    w = jnp.concatenate([other[j, 0:HALF, :] for j in range(4)], axis=1)
    total = pre[...] + jnp.dot(rest[...], w, preferred_element_type=F32)
    hidden = jax.nn.gelu(total).astype(BF16)
    for k, weights in enumerate((mine, other)):
        rows = []
        for j in range(4):
            cut = [HALF + i * BLOCK for i in range(3)]
            rows.append(jnp.concatenate([weights[j, r : r + BLOCK, :] for r in cut], axis=1))
        total = jnp.dot(hidden, jnp.concatenate(rows, axis=0), preferred_element_type=F32)
        cut = slice(k * 3 * BLOCK, (k + 1) * 3 * BLOCK)
        for j, step in enumerate((0, 3, 1, 2)):
            out[lax.rem(x + step, 4), :, cut] = total[j * ROWS : (j + 1) * ROWS].astype(BF16)


def query_kernel(partial, owner_row, rank_row, tags, out):
    line = iota((OWNERS * LINES, ROWS), 0)
    inner = line % LINES
    mine = (inner == LINES - 1) | (inner % CAP == rank_row[...])
    place = jnp.where(mine & (owner_row[...] == line // LINES), 1.0, 0.0).astype(BF16)
    proj = partial[0].astype(F32)
    for j in range(1, 4):
        proj = proj + partial[j].astype(F32)
    norm = jnp.sum(proj * proj, axis=1, keepdims=True)
    query = proj * (1.0 / jnp.sqrt(norm + EPS))
    low, high = query[:, 0 : EMB // 2], query[:, EMB // 2 :]
    straight = lax.axis_index("core") == 0
    query = jnp.concatenate(
        [jnp.where(straight, low, high), jnp.where(straight, high, low)], axis=1
    ).astype(BF16)
    total = jnp.dot(place, tags[...], preferred_element_type=F32)
    rows = jnp.dot(place, query, preferred_element_type=F32)
    chunk = iota((OWNERS * LINES, 1), 0) % LINES // CAP
    for k in range(3):
        total = jnp.where(chunk == k, rows[:, k * CHUNK : (k + 1) * CHUNK], total)
    out[...] = total.astype(BF16).reshape(OWNERS, LINES, CHUNK)


def join_kernel(low, high, out):
    rows = low.shape[0]
    out[0:rows, :] = low[...]
    out[rows:, :] = high[...]


def score_kernel(arrived, own, left, right, top, bottom, out, held, sem):
    copies = [
        pltpu.make_async_copy(top, held.at[0 : 2 * UNIT, :], sem.at[0]),
        pltpu.make_async_copy(bottom, held.at[2 * UNIT :, :], sem.at[1]),
    ]
    for copy in copies:
        copy.start()
    parts = (own, left, right, held)
    row = iota((4 * OWNERS * CAP, 1), 0)
    kind, slot = row // (OWNERS * CAP), row % (OWNERS * CAP)
    line = jnp.where(kind < 3, kind * CAP + slot // OWNERS, LINES - 1)
    target = slot % OWNERS * LINES + line
    pick = jnp.where(iota((4 * OWNERS * CAP, OWNERS * LINES), 1) == target, 1.0, 0.0).astype(BF16)
    flat = arrived[...].reshape(OWNERS * LINES, CHUNK)
    moved = jnp.dot(pick, flat, preferred_element_type=F32)
    count = OWNERS * CAP
    query = jnp.concatenate(
        [moved[k * count : (k + 1) * count].astype(BF16) for k in range(3)], axis=1
    )
    slot = iota((count, CHUNK), 0) // OWNERS
    tag = jnp.sum(
        jnp.where(iota((count, CHUNK), 1) == slot, moved[3 * count :], 0.0), axis=1, keepdims=True
    )
    best = jnp.full((count, 2 * SLOTS), -1.0, F32)
    where = [(part, i * UNIT) for part in parts for i in range(part.shape[0] // UNIT)]
    for j in range(0, 16, 2):
        if j == 12:
            for copy in copies:
                copy.wait()
        blocks, marks = [], []
        for part, row in where[j : j + 2]:
            blocks.append(part[row : row + SLOTS, :])
            marks.append(part[row + SLOTS : row + UNIT, 0:SLOTS].astype(F32)[0:1])
        scores = lax.dot_general(
            query,
            jnp.concatenate(blocks, axis=0),
            (((1,), (1,)), ((), ())),
            preferred_element_type=F32,
        )
        allowed = jnp.concatenate(marks, axis=1) == tag
        best = jnp.maximum(best, jnp.where(allowed, scores, -1.0))
    best = jnp.max(best, axis=1, keepdims=True)
    lane = iota((OWNERS, SLOTS), 1)
    result = jnp.zeros((OWNERS, SLOTS), F32)
    for s in range(CAP):
        result = jnp.where(lane == s, best[s * OWNERS : (s + 1) * OWNERS], result)
    out[...] = result


def answer_kernel(answers, owner_row, rank_row, out):
    mine = owner_row[...] == iota((OWNERS, ROWS), 0)
    total = jnp.zeros((1, ROWS), F32)
    for s in range(CAP):
        value = jnp.sum(jnp.where(mine, answers[:, s : s + 1], 0.0), axis=0, keepdims=True)
        total = jnp.where(rank_row[...] == s, value, total)
    out[...] = total


def shift(value, axis, step):
    return lax.ppermute(value, axis, [(i, (i + step) % 4) for i in range(4)])


def turn(value, move, turned):
    pairs = []
    for c in range(2):
        for y in range(4):
            for x in range(4):
                to = (y, move(x)) if (c == 1) == turned else (move(y), x)
                pairs.append((c * 16 + y * 4 + x, c * 16 + to[0] * 4 + to[1]))
    return lax.ppermute(value, ("core", "y", "x"), pairs)


def up(place):
    return (place + 1) % 4


def down(place):
    return (place + 3) % 4


HBM = pl.BlockSpec(memory_space=pltpu.HBM)
VMEM = pl.BlockSpec(memory_space=pltpu.VMEM)


def halved(*arrays):
    return pl.pallas_call(
        weights_kernel,
        out_shape=pltpu.VMEM((4, PACK, BLOCK), BF16),
        in_specs=[HBM] * 2,
        out_specs=VMEM,
        scratch_shapes=[
            pltpu.VMEM((HALF, BLOCK), BF16),
            pltpu.VMEM((BLOCK, 3 * BLOCK), BF16),
            pltpu.SemaphoreType.DMA((2,)),
        ],
        name="weights",
        compiler_params=PARAMS,
    )(*map(stay, arrays))


def normalised(*arrays):
    return pl.pallas_call(
        unit_kernel,
        out_shape=sds((UNIT, EMB), BF16),
        in_specs=[HBM] * 3,
        out_specs=VMEM,
        scratch_shapes=[
            pltpu.VMEM((SLOTS, EMB), BF16),
            pltpu.VMEM((1, SLOTS), I32),
            pltpu.VMEM((1, SLOTS), I32),
            pltpu.SemaphoreType.DMA((3,)),
        ],
        name="unit",
        compiler_params=PARAMS,
    )(*map(stay, arrays))


def first(*arrays):
    return pl.pallas_call(
        first_kernel,
        out_shape=(pltpu.VMEM((4 * ROWS, 4 * BLOCK), F32), pltpu.VMEM((4 * ROWS, HALF), BF16)),
        in_specs=[HBM] * 3 + [VMEM] * 3,
        out_specs=(VMEM, VMEM),
        scratch_shapes=[pltpu.VMEM((4 * ROWS, HID), BF16), pltpu.SemaphoreType.DMA((3,))],
        name="first",
        cost_estimate=pl.CostEstimate(flops=30 << 30, bytes_accessed=4 << 20, transcendentals=0),
        compiler_params=PARAMS,
    )(*arrays)


def joined(blocks, *parts):
    return call(join_kernel, sds((blocks * UNIT, EMB), BF16), "join")(*map(near, parts))


def near(value):
    return pltpu.with_memory_space_constraint(value, pltpu.VMEM)


def score(*arrays):
    return pl.pallas_call(
        score_kernel,
        out_shape=sds((OWNERS, SLOTS), F32),
        in_specs=[VMEM] * 4 + [HBM] * 2,
        out_specs=VMEM,
        scratch_shapes=[pltpu.VMEM((4 * UNIT, EMB), BF16), pltpu.SemaphoreType.DMA((2,))],
        name="score",
        compiler_params=PARAMS,
    )(*arrays)


def stay(value):
    return pltpu.with_memory_space_constraint(value, pltpu.HBM)


def swap(value):
    return lax.ppermute(value, "core", [(0, 1), (1, 0)])


def body(features, w_hidden, w_embed, members, doc_owner, doc_local, member_cluster, member_valid):
    dp = ("z", "core")
    mine = lax.all_to_all(near(halved(w_hidden, w_embed)), "y", 0, 0, tiled=True)
    docs = [shift(features, "x", 1), shift(features, "x", -1)]
    unit = normalised(members, member_cluster, member_valid)
    beside = turn(unit, lambda place: place ^ 1, False)
    cut = 48
    docs += [shift(docs[0][:cut], "x", 1), shift(docs[1][cut:], "x", -1)]

    start = lax.axis_index(("y", "x")) * ROWS
    owner = lax.dynamic_slice_in_dim(doc_owner[:, 0], start, ROWS, 0)
    local = lax.dynamic_slice_in_dim(doc_local, start, ROWS, 0)
    owner_row = owner.reshape(1, ROWS)
    tags, rank_row = call(
        slots_kernel,
        (
            sds((ROWS, CHUNK), BF16),
            sds((1, ROWS), I32),
        ),
        "slots",
    )(owner_row, owner.reshape(ROWS, 1), local.reshape(ROWS, 1))

    mine, tags, docs[:2], beside = lax.optimization_barrier((mine, tags, docs[:2], beside))
    pair = joined(2, unit, beside)
    opposite = turn(pair, lambda place: 3 - place, False)
    other = swap(mine)
    column = joined(4, pair, opposite)
    left, right = turn(column, up, True), turn(column, down, True)
    top, bottom = turn(left[: 2 * UNIT], up, True), turn(right[2 * UNIT :], down, True)
    columns = [column, left, right, top, bottom]
    pre, rest = first(*map(stay, (features, *docs[:2])), *map(near, docs[2:]), mine)
    partial = call(head_kernel, pltpu.VMEM((4, ROWS, EMB), BF16), "head")(near(pre), near(rest), mine, other)
    partial = lax.all_to_all(near(partial), "x", 0, 0, tiled=True)
    outgoing = call(query_kernel, pltpu.VMEM((OWNERS, LINES, CHUNK), BF16), "query")(
        partial, owner_row, rank_row, tags
    )
    arrived = lax.all_to_all(near(outgoing), dp, 0, 0, tiled=True)
    best = score(arrived, *map(near, columns[:3]), *map(stay, columns[3:]))
    answers = lax.all_to_all(best, dp, 0, 0, tiled=True)
    result = call(answer_kernel, sds((1, ROWS), F32), "answer")(answers, owner_row, rank_row)
    return result.reshape(ROWS)


def solution(mesh):
    grid = Mesh(mesh.devices.reshape(16, 2, 4, 4), ("z", "core", "y", "x"))
    dp, tensor = ("z", "core"), ("y", "x")
    every = dp + tensor
    return jax.shard_map(
        body,
        mesh=grid,
        in_specs=(
            P(every, None),
            P(None, tensor),
            P(tensor, None),
            P(dp, tensor, None),
            P(dp, None),
            P(dp),
            P(dp, tensor),
            P(dp, tensor),
        ),
        out_specs=P(every),
        check_vma=False,
    )
```
